128 devices in a mesh: dp: 2 (over core), expert: 64 (over z, y, x).
Axes of the slice: x: 4, y: 4, z: 4, core: 2. Of those that a mesh axis runs over, the one named last changes fastest.
Arguments:
- tokens: bfloat16 [16384, 2048], P(('dp', 'expert')), may hold values from -6 to 6
- cotangent: bfloat16 [16384, 2048], P(('dp', 'expert')), may hold values from -3 to 3
- experts: int32 [16384, 4], P(('dp', 'expert')), may hold values from 0 to 63, as said below
- mixing: float32 [16384, 4], P(('dp', 'expert')), may hold values from 0.1 to 0.9
- gate_matrix: bfloat16 [64, 2048, 768], P('expert'), may hold values from -0.125 to 0.125
- up_matrix: bfloat16 [64, 2048, 768], P('expert'), may hold values from -0.125 to 0.125
- down_matrix: bfloat16 [64, 768, 2048], P('expert'), may hold values from -0.21875 to 0.21875
Outputs:
- input_grad: bfloat16 [16384, 2048], P(('dp', 'expert'))
- gate_grad: float32 [64, 2048, 768], P('expert', 'dp')
- up_grad: float32 [64, 2048, 768], P('expert', 'dp')
- down_grad: float32 [64, 768, 2048], P('expert', 'dp')
The draws below stay inside these ranges and needn't reach their ends.
Inputs may be any that keep to these rules, and one draw needn't show every extreme that they name: A token names 4 different experts. Among the 128 tokens of one device, expert e and expert (e + 32) mod 64 are named together exactly 2 * 8 times, no expert more than 16 times, and one expert is named exactly 16 times by the tokens of every device.
All inputs are finite; a program needn't handle non-finite values.
Results may differ from the reference program's by a relative error of at most 0.0065.
Values may be sent and summed in bfloat16 or wider, within the bound.
A program may use at most 128 MiB of HBM per device.

```python
import jax
import jax.numpy as jnp
from jax import lax

D = 2048
FF = 768
TOP = 4
EXPERTS = 64
TOK_DEV = 128
TOKENS = 16384
LOAD = 8
CAP = 16
N_DP = 2
N_EXPERT = 64


def block_routes(block_key, hot_expert):
    key_delta, key_rows, key_cols = jax.random.split(block_key, 3)
    half_count = EXPERTS // 2
    deltas = jax.random.randint(key_delta, (half_count,), -LOAD, LOAD + 1, dtype=jnp.int32)
    hot_delta = jnp.where(hot_expert < half_count, LOAD, -LOAD).astype(jnp.int32)
    deltas = jnp.where(jnp.arange(half_count, dtype=jnp.int32) == hot_expert % half_count, hot_delta, deltas)
    counts = jnp.concatenate([LOAD + deltas, LOAD - deltas]).astype(jnp.int32)
    run_ends = jnp.cumsum(counts)
    places = jnp.arange(TOK_DEV * TOP, dtype=jnp.int32)
    listing = jnp.sum((run_ends[None, :] <= places[:, None]).astype(jnp.int32), axis=1)
    layout = listing.reshape(TOP, TOK_DEV).T
    row_order = jax.random.permutation(key_rows, TOK_DEV)
    layout = layout[row_order]
    col_scores = jax.random.randint(key_cols, (TOK_DEV, TOP), 0, 1 << 20, dtype=jnp.int32) * TOP + jnp.arange(TOP, dtype=jnp.int32)[None, :]
    col_order = jnp.argsort(col_scores, axis=1, stable=True)
    return jnp.take_along_axis(layout, col_order, axis=1)


def draw_experts(key, part):
    key_hot, key_blocks = jax.random.split(jax.random.fold_in(key, 7))
    hot_expert = jax.random.randint(key_hot, (), 0, EXPERTS, dtype=jnp.int32)
    block_keys = jax.random.split(key_blocks, TOKENS // TOK_DEV)
    routed = jax.vmap(lambda block_key: block_routes(block_key, hot_expert))(block_keys)
    return routed.reshape(TOKENS, TOP).astype(jnp.int32)


def steps_of(stream_key, extent, cuts, least, top_value):
    factor_of, own = 1.0, jax.random.fold_in(stream_key, 6)
    for dim, blocks in cuts:
        steps = jnp.exp(jax.random.uniform(jax.random.fold_in(own, dim), (blocks,), jnp.float32, least / len(cuts), top_value / len(cuts)))
        factor_of = factor_of * jnp.repeat(steps, extent[dim] // blocks).reshape([-1 if axis == dim else 1 for axis in range(len(extent))])
    return factor_of


def bell_draw(rng, dims, width, most, cuts=(), held_as=jnp.bfloat16):
    drawn = jax.random.normal(rng, dims, jnp.float32) * width
    if len(cuts) > 0:
        drawn = steps_of(rng, dims, cuts, -0.22, 0.18) * drawn
    return jnp.clip(drawn, min=-most, max=most).astype(held_as)


def setup_inputs(seed: int = 0) -> dict:
    seeds = jax.random.split(jax.random.key(seed), 8)
    tokens = bell_draw(seeds[0], (TOKENS, D), 1.0, 6.0, ((0, 128),))
    cotangent = bell_draw(seeds[1], (TOKENS, D), 0.5, 3.0, ((0, 128),))
    experts = draw_experts(jax.random.fold_in(seeds[7], 71), 0)
    mixing = jnp.clip(0.1 + 0.79999997 * jax.random.uniform(seeds[3], (TOKENS, TOP), jnp.float32) ** steps_of(seeds[3], (TOKENS, TOP), ((0, 128),), -0.2, 0.2), 0.1, 0.9)
    gate_matrix = bell_draw(seeds[4], (EXPERTS, D, FF), D ** -0.5, 0.125, ((0, 64),))
    up_matrix = bell_draw(seeds[5], (EXPERTS, D, FF), D ** -0.5, 0.125, ((0, 64),))
    down_matrix = bell_draw(seeds[6], (EXPERTS, FF, D), FF ** -0.5, 0.21875, ((0, 64),))
    return dict(tokens=tokens, cotangent=cotangent, experts=experts, mixing=mixing, gate_matrix=gate_matrix, up_matrix=up_matrix, down_matrix=down_matrix)


def build_table(experts):
    blocks = TOKENS // TOK_DEV
    per_block = TOK_DEV * TOP
    routed = experts.reshape(blocks, per_block)
    labels = jnp.arange(EXPERTS, dtype=jnp.int32)
    onehot = (routed[:, :, None] == labels[None, None, :]).astype(jnp.int32)
    position = jnp.sum(onehot * (jnp.cumsum(onehot, axis=1) - 1), axis=2)
    column = jnp.arange(blocks, dtype=jnp.int32)[:, None] * CAP + position
    pair_ids = jnp.arange(TOKENS * TOP, dtype=jnp.int32).reshape(blocks, per_block)
    empty_table = jnp.full((EXPERTS, blocks * CAP), TOKENS * TOP, dtype=jnp.int32)
    return empty_table.at[routed, column].set(pair_ids)


def round_back(values):
    rounded = lax.optimization_barrier(values.astype(jnp.bfloat16))
    return rounded.astype(jnp.float32)


def reference(tokens, cotangent, experts, mixing, gate_matrix, up_matrix, down_matrix):
    table = build_table(experts)
    flat_mixing = mixing.reshape(TOKENS * TOP)
    group_shape = (N_DP, N_EXPERT, 2, LOAD)

    def one_expert(accumulated, expert_items):
        table_row, weight_gate, weight_up, weight_down = expert_items
        live_rows = table_row < TOKENS * TOP
        safe_index = jnp.where(live_rows, table_row, 0)
        token_ids = safe_index // TOP
        inputs = jnp.where(live_rows[:, None], tokens[token_ids], jnp.zeros((), jnp.bfloat16))
        weight_row = jnp.where(live_rows, flat_mixing[safe_index], jnp.zeros((), jnp.float32))
        scaled = (weight_row[:, None] * cotangent[token_ids].astype(jnp.float32)).astype(jnp.bfloat16)
        pre_gate = jnp.dot(inputs, weight_gate, preferred_element_type=jnp.float32)
        pre_up = jnp.dot(inputs, weight_up, preferred_element_type=jnp.float32)
        sigmoid_gate = jax.nn.sigmoid(pre_gate)
        activated = pre_gate * sigmoid_gate
        hidden = (activated * pre_up).astype(jnp.bfloat16)
        hidden_cot = jnp.dot(scaled, weight_down.T, preferred_element_type=jnp.float32)
        gate_cot = (hidden_cot * pre_up * sigmoid_gate * (1.0 + pre_gate * (1.0 - sigmoid_gate))).astype(jnp.bfloat16)
        up_cot = (hidden_cot * activated).astype(jnp.bfloat16)
        pair_cot = (jnp.dot(gate_cot, weight_gate.T, preferred_element_type=jnp.float32)
                    + jnp.dot(up_cot, weight_up.T, preferred_element_type=jnp.float32)).astype(jnp.bfloat16)
        accumulated = accumulated.at[token_ids].add(
            jnp.where(live_rows[:, None], pair_cot.astype(jnp.float32), jnp.zeros((), jnp.float32)))
        grouped_in = inputs.astype(jnp.float32).reshape(group_shape + (D,))
        grouped_gate = gate_cot.astype(jnp.float32).reshape(group_shape + (FF,))
        grouped_up = up_cot.astype(jnp.float32).reshape(group_shape + (FF,))
        grouped_hidden = hidden.astype(jnp.float32).reshape(group_shape + (FF,))
        grouped_cot = scaled.astype(jnp.float32).reshape(group_shape + (D,))
        gate_part = jnp.einsum("djsrk,djsrf->dskf", grouped_in, grouped_gate)
        up_part = jnp.einsum("djsrk,djsrf->dskf", grouped_in, grouped_up)
        down_part = jnp.einsum("djsrf,djsrk->dsfk", grouped_hidden, grouped_cot)
        gate_sum = jnp.sum(gate_part[:, 0], axis=0) + jnp.sum(round_back(gate_part[:, 1]), axis=0)
        up_sum = jnp.sum(up_part[:, 0], axis=0) + jnp.sum(round_back(up_part[:, 1]), axis=0)
        down_sum = jnp.sum(down_part[:, 0], axis=0) + jnp.sum(round_back(down_part[:, 1]), axis=0)
        return accumulated, (gate_sum, up_sum, down_sum)

    zero_start = jnp.zeros((TOKENS, D), jnp.float32)
    summed, expert_grads = lax.scan(one_expert, zero_start, (table, gate_matrix, up_matrix, down_matrix))
    return summed.astype(jnp.bfloat16), expert_grads[0], expert_grads[1], expert_grads[2]
```

```python
import jax
import jax.numpy as jnp
from jax import lax
from jax.experimental import pallas as pl
from jax.experimental.pallas import tpu as pltpu
from jax.sharding import PartitionSpec as P

MESH = pl.DeviceIdType.MESH
BF = jnp.bfloat16
F32 = jnp.float32
SIDE = 4
ROWS = 16
NC = 8
TOK = 128
NT = (((1,), (1,)), ((), ()))
TN = (((0,), (0,)), ((), ()))


def ranks(meta):
    pair_label = lax.broadcasted_iota(jnp.int32, (32, TOK), 0).astype(F32)
    onehots, names = [], []
    for k in range(4):
        name = meta[k : k + 1, :]
        names.append(name)
        pair = jnp.where(name >= 32.0, name - 32.0, name)
        onehots.append((pair_label == pair).astype(F32))
    count = onehots[0] + onehots[1] + onehots[2] + onehots[3]
    before = (
        lax.broadcasted_iota(jnp.int32, (TOK, TOK), 0)
        < lax.broadcasted_iota(jnp.int32, (TOK, TOK), 1)
    ).astype(BF)
    seen = jnp.dot(count.astype(BF), before, preferred_element_type=F32)
    out = []
    for k in range(4):
        out.append(jnp.sum(onehots[k] * seen, axis=0, keepdims=True))
        seen = seen + onehots[k]
    return names, out


def kernel(
    meta_ref,
    tok_hbm,
    cot_hbm,
    wg_hbm,
    wu_hbm,
    wd_hbm,
    out_hbm,
    gg_hbm,
    ug_hbm,
    dg_hbm,
    tokv,
    meta_z,
    sel2,
    sel1,
    mix1,
    x2,
    b1,
    b2,
    xf,
    ag,
    dq,
    bq,
    cf,
    wg,
    wu,
    wd,
    acc,
    hid,
    gcot,
    ucot,
    hidden,
    rz,
    ry,
    rx,
    outv,
    pgu,
    pdn,
    qgu,
    qdn,
    dstage,
    in_sem,
    w_sem,
    loc_sem,
    m_s,
    m_r,
    snd,
    rcv,
    p_s,
    p_r,
    o_sem,
):
    fc = tokv.shape[2]
    ff = gcot.shape[1]
    half_ff = ff // 2
    d = lax.axis_index("dp")
    e = lax.axis_index("expert")
    z = lax.div(e, 16)
    y = lax.rem(lax.div(e, 4), 4)
    x = lax.rem(e, 4)
    other = 1 - d

    def at_z(v):
        return (d, v * 16 + y * 4 + x)

    def at_y(v):
        return (d, z * 16 + v * 4 + x)

    def at_x(v):
        return (d, z * 16 + y * 4 + v)

    def step(v, j):
        return lax.rem(v + j, SIDE)

    def remote(src, dst, ssem, rsem, dev):
        return pltpu.make_async_remote_copy(
            src_ref=src, dst_ref=dst, send_sem=ssem, recv_sem=rsem, device_id=dev, device_id_type=MESH
        )

    def xx(c, j):
        v = step(x, j)
        return remote(x2.at[c, v], b1.at[c, x], snd.at[0, c, j - 1], rcv.at[0, c, j - 1], at_x(v))

    def xy(c, j):
        v = step(y, j)
        return remote(b1.at[c, :, v], b2.at[c, y], snd.at[1, c, j - 1], rcv.at[1, c, j - 1], at_y(v))

    def xz(c, j):
        v = step(z, j)
        return remote(
            b2.at[c, :, :, lax.rem(v, 2)], xf.at[c, z], snd.at[2, c, j - 1], rcv.at[2, c, j - 1], at_z(v)
        )

    def cz(c, j):
        v = step(z, j)
        return remote(ag.at[c, z], ag.at[c, z], snd.at[3, c, j - 1], rcv.at[3, c, j - 1], at_z(v))

    def cy(c, j):
        v = step(y, j)
        return remote(
            dq.at[lax.rem(c, 2), v], bq.at[c, :, y], snd.at[4, c, j - 1], rcv.at[4, c, j - 1], at_y(v)
        )

    def cx(c, j):
        v = step(x, j)
        return remote(
            bq.at[c, :, :, v], cf.at[c, :, :, x], snd.at[5, c, j - 1], rcv.at[5, c, j - 1], at_x(v)
        )

    def rzc(c, j):
        v = step(z, j)
        return remote(bq.at[c, v], rz.at[c, j - 1], snd.at[6, c, j - 1], rcv.at[6, c, j - 1], at_z(v))

    def ryc(c, j):
        v = step(y, j)
        return remote(b1.at[c, v], ry.at[c, y], snd.at[7, c, j - 1], rcv.at[7, c, j - 1], at_y(v))

    def rxc(c, j):
        v = step(x, j)
        return remote(ry.at[c, :, v], rx.at[c, x], snd.at[8, c, j - 1], rcv.at[8, c, j - 1], at_x(v))

    def mz(j):
        return remote(meta_z.at[z], meta_z.at[z], m_s.at[j - 1], m_r.at[j - 1], at_z(step(z, j)))

    def start(copy, c):
        for j in (1, 3, 2):
            copy(c, j).start()

    def arrive(copy, c):
        for j in (1, 3, 2):
            copy(c, j).wait_recv()

    def sent(copy, c):
        for j in (1, 3, 2):
            copy(c, j).wait_send()

    def own(i, c):
        src, dst = (
            (x2.at[c, x], b1.at[c, x]),
            (b1.at[c, :, y], b2.at[c, y]),
            (b2.at[c, :, :, lax.rem(z, 2)], xf.at[c, z]),
            (dq.at[lax.rem(c, 2), y], bq.at[c, :, y]),
            (bq.at[c, :, :, x], cf.at[c, :, :, x]),
            (b1.at[c, y], ry.at[c, y]),
            (ry.at[c, :, x], rx.at[c, x]),
        )[i]
        return pltpu.make_async_copy(src, dst, loc_sem.at[i, c])

    def tok_in(c):
        cols = pl.ds(pl.multiple_of(c * fc, fc), fc)
        return pltpu.make_async_copy(tok_hbm.at[:, cols], tokv.at[c], in_sem.at[0, c])

    def cot_in(c):
        cols = pl.ds(pl.multiple_of(c * fc, fc), fc)
        return pltpu.make_async_copy(cot_hbm.at[:, cols], ag.at[c, z], in_sem.at[1, c])

    weights_in = [
        pltpu.make_async_copy(wg_hbm.at[0], wg, w_sem.at[0]),
        pltpu.make_async_copy(wu_hbm.at[0], wu, w_sem.at[1]),
        pltpu.make_async_copy(wd_hbm.at[0], wd, w_sem.at[2]),
    ]
    meta_in = pltpu.make_async_copy(meta_ref, meta_z.at[z], w_sem.at[3])

    meta_in.start()

    @pl.loop(0, NC)
    def _(c):
        cot_in(c).start()
        tok_in(c).start()

    for copy in weights_in:
        copy.start()

    barrier = pltpu.get_barrier_semaphore()
    for j in (1, 2, 3):
        for dev in (at_x(step(x, j)), at_y(step(y, j)), at_z(step(z, j))):
            pl.semaphore_signal(barrier, inc=1, device_id=dev, device_id_type=MESH)
    pl.semaphore_signal(barrier, inc=1, device_id=(other, e), device_id_type=MESH)

    meta_in.wait()
    names, rank = ranks(meta_ref[...])
    slots = []
    for k in range(4):
        pair = jnp.where(names[k] >= 32.0, names[k] - 32.0, names[k])
        high = (pair >= 16.0).astype(F32)
        rest = pair - 16.0 * high
        row = jnp.floor(rest * 0.25)
        slots.append(((rest - 4.0 * row) * 8.0 + row * 2.0 + high) * ROWS + rank[k])
    slot_label = lax.broadcasted_iota(jnp.int32, (512, TOK), 0).astype(F32)
    picked = (slot_label == slots[0]).astype(F32)
    for k in range(1, 4):
        picked = picked + (slot_label == slots[k]).astype(F32)
    sel2[...] = picked.astype(BF)

    pl.semaphore_wait(barrier, 10)
    for j in (1, 3, 2):
        mz(j).start()

    @pl.loop(0, NC)
    def _(c):
        cot_in(c).wait()
        start(cz, c)
        tok_in(c).wait()
        rows = jnp.dot(sel2[...], tokv[c], preferred_element_type=F32).astype(BF)
        x2[c] = rows.reshape(SIDE, SIDE, 2, ROWS, fc)
        start(xx, c)
        own(0, c).start()

    for j in (1, 3, 2):
        mz(j).wait_recv()
    plane = z.astype(F32) * 16.0
    label1 = lax.broadcasted_iota(jnp.int32, (256, TOK), 0).astype(F32)
    for s in range(SIDE):
        names_s, rank_s = ranks(meta_z[s])
        picked = jnp.zeros((256, TOK), F32)
        mixed = jnp.zeros((256, TOK), F32)
        for k in range(4):
            hit = label1 == (names_s[k] - plane) * ROWS + rank_s[k]
            picked = picked + hit.astype(F32)
            mixed = mixed + jnp.where(hit, meta_z[s, 4 + k : 5 + k, :], 0.0)
        sel1[s] = picked.astype(BF)
        mix1[s] = jnp.sum(mixed, axis=1, keepdims=True)

    acc[...] = jnp.zeros_like(acc)
    hid[...] = jnp.zeros_like(hid)
    for copy in weights_in:
        copy.wait()

    @pl.loop(0, NC + 2)
    def _(it):
        @pl.when(it < NC)
        def _():
            c = it
            arrive(xx, c)
            own(0, c).wait()
            start(xy, c)
            own(1, c).start()
            arrive(cz, c)

            @pl.when(c >= 2)
            def _():
                sent(cy, c - 2)

            for s in range(SIDE):
                rows = jnp.dot(sel1[s], ag[c, s], preferred_element_type=F32) * mix1[s]
                dq[lax.rem(c, 2), :, s] = rows.astype(BF).reshape(SIDE, SIDE, ROWS, fc)
            start(cy, c)
            own(3, c).start()

        @pl.when((it >= 1) & (it <= NC))
        def _():
            c = it - 1
            arrive(xy, c)
            own(1, c).wait()
            start(xz, c)
            own(2, c).start()
            arrive(cy, c)

            own(3, c).wait()
            start(cx, c)
            own(4, c).start()

        @pl.when(it >= 2)
        def _():
            c = it - 2
            feats = pl.ds(pl.multiple_of(c * fc, fc), fc)
            arrive(xz, c)
            own(2, c).wait()

            @pl.loop(0, SIDE)
            def _(s):
                rows = pl.ds(pl.multiple_of(s * 256, 256), 256)
                block = xf[c, s].reshape(256, fc)
                acc[rows, 0:ff] += jnp.dot(block, wg[feats, :], preferred_element_type=F32)
                acc[rows, ff : 2 * ff] += jnp.dot(block, wu[feats, :], preferred_element_type=F32)

            arrive(cx, c)
            own(4, c).wait()

            @pl.loop(0, SIDE)
            def _(s):
                rows = pl.ds(pl.multiple_of(s * 256, 256), 256)
                block = cf[c, s].reshape(256, fc)
                hid[rows, :] += lax.dot_general(
                    block, wd[:, feats], NT, preferred_element_type=F32
                )

    @pl.loop(0, 1024 // 32)
    def _(i):
        rows = pl.ds(pl.multiple_of(i * 32, 32), 32)
        pre_gate = acc[rows, 0:ff]
        pre_up = acc[rows, ff : 2 * ff]
        hidden_cot = hid[rows, :]
        sigmoid_gate = jax.nn.sigmoid(pre_gate)
        activated = pre_gate * sigmoid_gate
        hidden[rows, :] = (activated * pre_up).astype(BF)
        gcot[rows, :] = (
            hidden_cot * pre_up * sigmoid_gate * (1.0 + pre_gate * (1.0 - sigmoid_gate))
        ).astype(BF)
        ucot[rows, :] = (hidden_cot * activated).astype(BF)

    @pl.loop(0, NC)
    def _(c):
        sent(xx, c)
        sent(xy, c)
        sent(xz, c)
        sent(cz, c)
        sent(cx, c)

    for c in (NC - 2, NC - 1):
        sent(cy, c)
    for j in (1, 3, 2):
        mz(j).wait_send()

    own_half = lax.rem(z, 2)
    far_half = 1 - own_half

    def gu_send(j):
        return remote(pgu.at[lax.rem(j, 2)], qgu.at[j], p_s.at[0, j], p_r.at[0, j], (other, e))

    def dn_send(j):
        return remote(pdn.at[lax.rem(j, 2)], qdn.at[j], p_s.at[1, j], p_r.at[1, j], (other, e))

    def grads(j, side, store_gu, store_dn):
        c = side * (NC // 2) + j
        left = xf[c].reshape(1024, fc)
        store_gu(0, lax.dot_general(left, gcot[...], TN, preferred_element_type=F32))
        store_gu(1, lax.dot_general(left, ucot[...], TN, preferred_element_type=F32))
        units = pl.ds(pl.multiple_of(side * half_ff, 128), half_ff)
        for b in range(2):
            right = cf[2 * j + b].reshape(1024, fc)
            store_dn(
                b, lax.dot_general(hidden[:, units], right, TN, preferred_element_type=F32)
            )

    def gg_out(j):
        rows = pl.ds(pl.multiple_of(j * fc, fc), fc)
        return pltpu.make_async_copy(acc.at[rows, 0:ff], gg_hbm.at[0, rows, :], o_sem.at[0, j])

    def ug_out(j):
        rows = pl.ds(pl.multiple_of(j * fc, fc), fc)
        return pltpu.make_async_copy(acc.at[rows, ff : 2 * ff], ug_hbm.at[0, rows, :], o_sem.at[1, j])

    def dg_out(j):
        cols = pl.ds(pl.multiple_of(j * 2 * fc, 2 * fc), 2 * fc)
        return pltpu.make_async_copy(dstage.at[lax.rem(j, 2)], dg_hbm.at[0, :, cols], o_sem.at[2, j])

    @pl.loop(0, NC + 3)
    def _(it):
        @pl.when(it < NC)
        def _():
            c = it
            feats = pl.ds(pl.multiple_of(c * fc, fc), fc)

            @pl.loop(0, SIDE)
            def _(s):
                rows = pl.ds(pl.multiple_of(s * 256, 256), 256)
                back = lax.dot_general(
                    gcot[rows, :], wg[feats, :], NT, preferred_element_type=F32
                ) + lax.dot_general(ucot[rows, :], wu[feats, :], NT, preferred_element_type=F32)
                bq[c, s] = back.astype(BF).reshape(SIDE, SIDE, ROWS, fc)

            start(rzc, c)

        @pl.when(it < NC // 2)
        def _():
            j = it

            @pl.when(j >= 2)
            def _():
                gu_send(j - 2).wait_send()
                dn_send(j - 2).wait_send()

            def store_gu(which, value):
                pgu[lax.rem(j, 2), :, which * ff : (which + 1) * ff] = value.astype(BF)

            def store_dn(b, value):
                pdn[lax.rem(j, 2), :, b * fc : (b + 1) * fc] = value.astype(BF)

            grads(j, other, store_gu, store_dn)
            gu_send(j).start()
            dn_send(j).start()

        @pl.when((it >= NC // 2) & (it < NC))
        def _():
            j = it - NC // 2
            gu_send(j).wait_recv()
            dn_send(j).wait_recv()

            @pl.when(j >= 2)
            def _():
                dg_out(j - 2).wait()

            rows = pl.ds(pl.multiple_of(j * fc, fc), fc)

            def store_gu(which, value):
                cols = slice(which * ff, (which + 1) * ff)
                acc[rows, cols] = value + qgu[j, :, cols].astype(F32)

            def store_dn(b, value):
                cols = slice(b * fc, (b + 1) * fc)
                dstage[lax.rem(j, 2), :, cols] = value + qdn[j, :, cols].astype(F32)

            grads(j, d, store_gu, store_dn)
            gg_out(j).start()
            ug_out(j).start()
            dg_out(j).start()

        @pl.when((it >= 1) & (it <= NC))
        def _():
            c = it - 1
            arrive(rzc, c)
            b1[c, :, :, own_half] = bq[c, z] + rz[c, 1]
            b1[c, :, :, far_half] = rz[c, 0] + rz[c, 2]
            start(ryc, c)
            own(5, c).start()

        @pl.when((it >= 2) & (it <= NC + 1))
        def _():
            c = it - 2
            arrive(ryc, c)
            own(5, c).wait()
            start(rxc, c)
            own(6, c).start()

        @pl.when(it >= 3)
        def _():
            c = it - 3
            arrive(rxc, c)
            own(6, c).wait()
            cols = pl.ds(pl.multiple_of(c * fc, fc), fc)
            outv[:, cols] = lax.dot_general(
                sel2[...], rx[c].reshape(512, fc), TN, preferred_element_type=F32
            ).astype(BF)

    result = pltpu.make_async_copy(outv, out_hbm, w_sem.at[3])
    result.start()

    @pl.loop(0, NC)
    def _(c):
        sent(rzc, c)
        sent(ryc, c)
        sent(rxc, c)

    for j in (NC // 2 - 2, NC // 2 - 1):
        gu_send(j).wait_send()
        dn_send(j).wait_send()
        dg_out(j).wait()
    for j in range(NC // 2):
        gg_out(j).wait()
        ug_out(j).wait()
    result.wait()


def local(tokens, cotangent, experts, mixing, gate_matrix, up_matrix, down_matrix):
    width = tokens.shape[1]
    ff = gate_matrix.shape[2]
    fc = width // NC
    meta = jnp.concatenate([experts.T.astype(F32), mixing.T], axis=0)
    anywhere = pl.BlockSpec(memory_space=pl.ANY)
    pair_rows = (NC, SIDE, SIDE, 2, ROWS, fc)
    all_rows = (NC, SIDE, SIDE, SIDE, ROWS, fc)
    return pl.pallas_call(
        kernel,
        out_shape=(
            jax.ShapeDtypeStruct((TOK, width), BF),
            jax.ShapeDtypeStruct((1, width // 2, ff), F32),
            jax.ShapeDtypeStruct((1, width // 2, ff), F32),
            jax.ShapeDtypeStruct((1, ff // 2, width), F32),
        ),
        in_specs=[pl.BlockSpec(memory_space=pltpu.VMEM)] + [anywhere] * 5,
        out_specs=(anywhere,) * 4,
        scratch_shapes=[
            pltpu.VMEM((NC, TOK, fc), BF),
            pltpu.VMEM((SIDE, 8, TOK), F32),
            pltpu.VMEM((512, TOK), BF),
            pltpu.VMEM((SIDE, 256, TOK), BF),
            pltpu.VMEM((SIDE, 256, 1), F32),
            pltpu.VMEM(pair_rows, BF),
            pltpu.VMEM(pair_rows, BF),
            pltpu.VMEM(pair_rows, BF),
            pltpu.VMEM(all_rows, BF),
            pltpu.VMEM((NC, SIDE, TOK, fc), BF),
            pltpu.VMEM((2, SIDE, SIDE, SIDE, ROWS, fc), BF),
            pltpu.VMEM(all_rows, BF),
            pltpu.VMEM(all_rows, BF),
            pltpu.VMEM((width, ff), BF),
            pltpu.VMEM((width, ff), BF),
            pltpu.VMEM((ff, width), BF),
            pltpu.VMEM((1024, 2 * ff), F32),
            pltpu.VMEM((1024, ff), F32),
            pltpu.VMEM((1024, ff), BF),
            pltpu.VMEM((1024, ff), BF),
            pltpu.VMEM((1024, ff), BF),
            pltpu.VMEM((NC, 3, SIDE, SIDE, ROWS, fc), BF),
            pltpu.VMEM(pair_rows, BF),
            pltpu.VMEM(pair_rows, BF),
            pltpu.VMEM((TOK, width), BF),
            pltpu.VMEM((2, fc, 2 * ff), BF),
            pltpu.VMEM((2, ff // 2, 2 * fc), BF),
            pltpu.VMEM((NC // 2, fc, 2 * ff), BF),
            pltpu.VMEM((NC // 2, ff // 2, 2 * fc), BF),
            pltpu.VMEM((2, ff // 2, 2 * fc), F32),
            pltpu.SemaphoreType.DMA((2, NC)),
            pltpu.SemaphoreType.DMA((4,)),
            pltpu.SemaphoreType.DMA((7, NC)),
            pltpu.SemaphoreType.DMA((3,)),
            pltpu.SemaphoreType.DMA((3,)),
            pltpu.SemaphoreType.DMA((9, NC, 3)),
            pltpu.SemaphoreType.DMA((9, NC, 3)),
            pltpu.SemaphoreType.DMA((2, NC // 2)),
            pltpu.SemaphoreType.DMA((2, NC // 2)),
            pltpu.SemaphoreType.DMA((3, NC // 2)),
        ],
        compiler_params=pltpu.CompilerParams(
            collective_id=0, has_side_effects=True, vmem_limit_bytes=67043328
        ),
    )(meta, tokens, cotangent, gate_matrix, up_matrix, down_matrix)


def solution(mesh):
    return jax.shard_map(
        local,
        mesh=mesh,
        in_specs=(
            P(("dp", "expert"), None),
            P(("dp", "expert"), None),
            P(("dp", "expert"), None),
            P(("dp", "expert"), None),
            P("expert", None, None),
            P("expert", None, None),
            P("expert", None, None),
        ),
        out_specs=(
            P(("dp", "expert"), None),
            P("expert", "dp", None),
            P("expert", "dp", None),
            P("expert", "dp", None),
        ),
        check_vma=False,
    )
```

```python
import jax
import jax.numpy as jnp
from jax import lax
from jax.experimental import pallas as pl
from jax.experimental.pallas import tpu as pltpu
from jax.sharding import PartitionSpec as P

MESH = pl.DeviceIdType.MESH
BF = jnp.bfloat16
F32 = jnp.float32
SIDE = 4
ROWS = 16
NC = 8
HC = NC // 2
SLOTS = 3
LAG1 = 2
LAG2 = 3
TOK = 128
NT = (((1,), (1,)), ((), ()))
TN = (((0,), (0,)), ((), ()))


def ranks(meta):
    pair_label = lax.broadcasted_iota(jnp.int32, (32, TOK), 0).astype(F32)
    onehots, names = [], []
    for k in range(4):
        name = meta[k : k + 1, :]
        names.append(name)
        pair = jnp.where(name >= 32.0, name - 32.0, name)
        onehots.append((pair_label == pair).astype(F32))
    count = onehots[0] + onehots[1] + onehots[2] + onehots[3]
    before = (
        lax.broadcasted_iota(jnp.int32, (TOK, TOK), 0)
        < lax.broadcasted_iota(jnp.int32, (TOK, TOK), 1)
    ).astype(BF)
    seen = jnp.dot(count.astype(BF), before, preferred_element_type=F32)
    out = []
    for k in range(4):
        out.append(jnp.sum(onehots[k] * seen, axis=0, keepdims=True))
        seen = seen + onehots[k]
    return names, out


def kernel(
    ids_ref,
    mix_ref,
    tok_hbm,
    cot_hbm,
    wg_hbm,
    wu_hbm,
    wd_hbm,
    out_hbm,
    gg_hbm,
    ug_hbm,
    dg_hbm,
    tokv,
    meta_z,
    sel2,
    sel1,
    mix1,
    x2,
    b1,
    b2,
    xf,
    ag,
    dq,
    bq,
    cf,
    wg,
    wu,
    wd,
    acc,
    hid,
    gcot,
    ucot,
    hidden,
    rz,
    ry,
    rx,
    t1,
    t2,
    pr,
    pgu,
    pdn,
    qgu,
    qdn,
    dstage,
    in_sem,
    w_sem,
    loc_sem,
    m_s,
    m_r,
    snd,
    rcv,
    p_s,
    p_r,
    o_sem,
):
    fc = tokv.shape[2]
    ff = gcot.shape[1]
    half_ff = ff // 2
    d = lax.axis_index("dp")
    e = lax.axis_index("expert")
    z = lax.div(e, 16)
    y = lax.rem(lax.div(e, 4), 4)
    x = lax.rem(e, 4)
    other = 1 - d

    def at_z(v):
        return (d, v * 16 + y * 4 + x)

    def at_y(v):
        return (d, z * 16 + v * 4 + x)

    def at_x(v):
        return (d, z * 16 + y * 4 + v)

    def step(v, j):
        return lax.rem(v + j, SIDE)

    def slot(c):
        return lax.rem(c, SLOTS)

    def remote(src, dst, ssem, rsem, dev):
        return pltpu.make_async_remote_copy(
            src_ref=src, dst_ref=dst, send_sem=ssem, recv_sem=rsem, device_id=dev, device_id_type=MESH
        )

    def x_first(c, par):
        if par == 0:
            return x, at_x, lambda v: x2.at[c, v], b1.at[c, x]
        return y, at_y, lambda v: x2.at[c, :, v], b1.at[c, y]

    def x_second(c, par):
        if par == 0:
            return y, at_y, lambda v: b1.at[c, :, v], b2.at[c, y]
        return x, at_x, lambda v: b1.at[c, :, v], b2.at[c, :, x]

    def x_third(c, par):
        return z, at_z, lambda v: b2.at[c, :, :, lax.rem(v, 2)], xf.at[c, z]

    def c_first(c, par):
        return z, at_z, lambda v: ag.at[c, z], ag.at[c, z]

    def c_second(c, par):
        if par == 0:
            return y, at_y, lambda v: dq.at[slot(c), v], bq.at[c, :, y]
        return x, at_x, lambda v: dq.at[slot(c), v], bq.at[c, :, x]

    def c_third(c, par):
        if par == 0:
            return x, at_x, lambda v: bq.at[c, :, :, v], cf.at[c, :, :, x]
        return y, at_y, lambda v: bq.at[c, :, :, v], cf.at[c, :, y]

    def r_second(k, par):
        if par == 0:
            return y, at_y, lambda v: b1.at[k, v], ry.at[k, y]
        return x, at_x, lambda v: b1.at[k, :, v], ry.at[k, x]

    def r_third(k, par):
        if par == 0:
            return x, at_x, lambda v: ry.at[k, :, v], rx.at[k, x]
        return y, at_y, lambda v: ry.at[k, :, v], rx.at[k, :, y]

    def t_first(k, par):
        if par == 0:
            return x, at_x, lambda v: bq.at[HC + k, :, :, v], t1.at[k, :, x]
        return y, at_y, lambda v: bq.at[HC + k, :, v], t1.at[k, :, y]

    def t_second(k, par):
        if par == 0:
            return y, at_y, lambda v: t1.at[k, :, :, v], t2.at[k, :, y]
        return x, at_x, lambda v: t1.at[k, :, :, v], t2.at[k, :, :, x]

    hops = [x_first, x_second, x_third, c_first, c_second, c_third, r_second, r_third, t_first, t_second]

    def copy_of(hop, c, par, j):
        i = hops.index(hop)
        here, at, src, dst = hop(c, par)
        v = step(here, j)
        return remote(src(v), dst, snd.at[i, c, j - 1], rcv.at[i, c, j - 1], at(v))

    def own_copy(hop, c, par):
        here, _, src, dst = hop(c, par)
        return pltpu.make_async_copy(src(here), dst, loc_sem.at[hops.index(hop), c])

    def start(hop, c, par):
        for j in (1, 3, 2):
            copy_of(hop, c, par, j).start()
        if hop is not c_first:
            own_copy(hop, c, par).start()

    def arrive(hop, c, par):
        for j in (1, 3, 2):
            copy_of(hop, c, par, j).wait_recv()
        if hop is not c_first:
            own_copy(hop, c, par).wait()

    def sent(hop, c, par):
        for j in (1, 3, 2):
            copy_of(hop, c, par, j).wait_send()

    def r_first(k, j):
        v = step(z, j)
        i = len(hops)
        return remote(bq.at[k, v], rz.at[k, j - 1], snd.at[i, k, j - 1], rcv.at[i, k, j - 1], at_z(v))

    def t_third(k, j):
        v = step(z, j)
        i = len(hops) + 1
        return remote(ag.at[k, v], pr.at[k, j - 1], snd.at[i, k, j - 1], rcv.at[i, k, j - 1], at_z(v))

    def mz(j):
        return remote(meta_z.at[z], meta_z.at[z], m_s.at[j - 1], m_r.at[j - 1], at_z(step(z, j)))

    def tok_in(c):
        cols = pl.ds(pl.multiple_of(c * fc, fc), fc)
        return pltpu.make_async_copy(tok_hbm.at[:, cols], tokv.at[c], in_sem.at[0, c])

    def tok_out(c):
        cols = pl.ds(pl.multiple_of(c * fc, fc), fc)
        return pltpu.make_async_copy(tokv.at[c], out_hbm.at[:, cols], in_sem.at[0, c])

    def cot_in(c):
        cols = pl.ds(pl.multiple_of(c * fc, fc), fc)
        return pltpu.make_async_copy(cot_hbm.at[:, cols], ag.at[c, z], in_sem.at[1, c])

    weights_in = [
        pltpu.make_async_copy(wg_hbm.at[0], wg, w_sem.at[0]),
        pltpu.make_async_copy(wu_hbm.at[0], wu, w_sem.at[1]),
        pltpu.make_async_copy(wd_hbm.at[0], wd, w_sem.at[2]),
    ]

    @pl.loop(0, NC)
    def _(c):
        cot_in(c).start()
        tok_in(c).start()

    for copy in weights_in:
        copy.start()

    barrier = pltpu.get_barrier_semaphore()
    for j in (1, 2, 3):
        for dev in (at_x(step(x, j)), at_y(step(y, j)), at_z(step(z, j))):
            pl.semaphore_signal(barrier, inc=1, device_id=dev, device_id_type=MESH)
    pl.semaphore_signal(barrier, inc=1, device_id=(other, e), device_id_type=MESH)

    meta_z[z, 0:4, :] = ids_ref[...].astype(F32)
    meta_z[z, 4:8, :] = mix_ref[...]
    names, rank = ranks(ids_ref[...].astype(F32))
    slots = []
    for k in range(4):
        pair = jnp.where(names[k] >= 32.0, names[k] - 32.0, names[k])
        high = (pair >= 16.0).astype(F32)
        rest = pair - 16.0 * high
        row = jnp.floor(rest * 0.25)
        slots.append(((rest - 4.0 * row) * 8.0 + row * 2.0 + high) * ROWS + rank[k])
    slot_label = lax.broadcasted_iota(jnp.int32, (512, TOK), 0).astype(F32)
    picked = (slot_label == slots[0]).astype(F32)
    for k in range(1, 4):
        picked = picked + (slot_label == slots[k]).astype(F32)
    sel2[...] = picked.astype(BF)

    pl.semaphore_wait(barrier, 10)
    for j in (1, 3, 2):
        mz(j).start()

    @pl.loop(0, HC)
    def _(i):
        for par in range(2):
            c = 2 * i + par
            cot_in(c).wait()
            start(c_first, c, par)
            tok_in(c).wait()
            rows = jnp.dot(sel2[...], tokv[c], preferred_element_type=F32).astype(BF)
            x2[c] = rows.reshape(SIDE, SIDE, 2, ROWS, fc)
            start(x_first, c, par)

    for j in (1, 3, 2):
        mz(j).wait_recv()
    plane = z.astype(F32) * 16.0
    label1 = lax.broadcasted_iota(jnp.int32, (256, TOK), 0).astype(F32)
    for s in range(SIDE):
        names_s, rank_s = ranks(meta_z[s])
        picked = jnp.zeros((256, TOK), F32)
        mixed = jnp.zeros((256, TOK), F32)
        for k in range(4):
            hit = label1 == (names_s[k] - plane) * ROWS + rank_s[k]
            picked = picked + hit.astype(F32)
            mixed = mixed + jnp.where(hit, meta_z[s, 4 + k : 5 + k, :], 0.0)
        sel1[s] = picked.astype(BF)
        mix1[s] = jnp.sum(mixed, axis=1, keepdims=True)

    acc[...] = jnp.zeros_like(acc)
    hid[...] = jnp.zeros_like(hid)
    for copy in weights_in:
        copy.wait()

    def second_hops(c, par):
        arrive(x_first, c, par)
        start(x_second, c, par)
        arrive(c_first, c, par)

        @pl.when(c >= SLOTS)
        def _():
            sent(c_second, c - SLOTS, (par + SLOTS) % 2)

        for s in range(SIDE):
            rows = jnp.dot(sel1[s], ag[c, s], preferred_element_type=F32) * mix1[s]
            rows = rows.astype(BF).reshape(SIDE, SIDE, ROWS, fc)
            if par == 0:
                dq[slot(c), :, s] = rows
            else:
                for v in range(SIDE):
                    dq[slot(c), :, s, v] = rows[v]
        start(c_second, c, par)

    def third_hops(c, par):
        arrive(x_second, c, par)
        start(x_third, c, par)
        arrive(c_second, c, par)
        start(c_third, c, par)

    def multiply(c, par):
        feats = pl.ds(pl.multiple_of(c * fc, fc), fc)
        arrive(x_third, c, par)

        @pl.loop(0, SIDE)
        def _(s):
            rows = pl.ds(pl.multiple_of(s * 256, 256), 256)
            block = xf[c, s].reshape(256, fc)
            acc[rows, 0:ff] += jnp.dot(block, wg[feats, :], preferred_element_type=F32)
            acc[rows, ff : 2 * ff] += jnp.dot(block, wu[feats, :], preferred_element_type=F32)

        arrive(c_third, c, par)

        @pl.loop(0, SIDE)
        def _(s):
            rows = pl.ds(pl.multiple_of(s * 256, 256), 256)
            block = cf[c, s].reshape(256, fc)
            hid[rows, :] += lax.dot_general(block, wd[:, feats], NT, preferred_element_type=F32)

    @pl.loop(0, HC + 2)
    def _(i):
        for par in range(2):
            it = 2 * i + par
            for lag, work in ((0, second_hops), (LAG1, third_hops), (LAG2, multiply)):

                @pl.when((it >= lag) & (it < NC + lag))
                def _():
                    work(it - lag, (par + lag) % 2)

    @pl.loop(0, 1024 // 32)
    def _(i):
        rows = pl.ds(pl.multiple_of(i * 32, 32), 32)
        pre_gate = acc[rows, 0:ff]
        pre_up = acc[rows, ff : 2 * ff]
        hidden_cot = hid[rows, :]
        sigmoid_gate = jax.nn.sigmoid(pre_gate)
        activated = pre_gate * sigmoid_gate
        hidden[rows, :] = (activated * pre_up).astype(BF)
        gcot[rows, :] = (
            hidden_cot * pre_up * sigmoid_gate * (1.0 + pre_gate * (1.0 - sigmoid_gate))
        ).astype(BF)
        ucot[rows, :] = (hidden_cot * activated).astype(BF)

    @pl.loop(0, HC)
    def _(i):
        for par in range(2):
            c = 2 * i + par
            for hop in (x_first, x_second, x_third, c_first, c_third):
                sent(hop, c, par)

    for c in range(NC - SLOTS, NC):
        sent(c_second, c, c % 2)
    for j in (1, 3, 2):
        mz(j).wait_send()

    own_half = lax.rem(z, 2)
    far_half = 1 - own_half

    def gu_send(j):
        return remote(pgu.at[lax.rem(j, 2)], qgu.at[j], p_s.at[0, j], p_r.at[0, j], (other, e))

    def dn_send(j):
        return remote(pdn.at[lax.rem(j, 2)], qdn.at[j], p_s.at[1, j], p_r.at[1, j], (other, e))

    def grads(j, side, store_gu, store_dn):
        c = side * HC + j
        left = xf[c].reshape(1024, fc)
        store_gu(0, lax.dot_general(left, gcot[...], TN, preferred_element_type=F32))
        store_gu(1, lax.dot_general(left, ucot[...], TN, preferred_element_type=F32))
        units = pl.ds(pl.multiple_of(side * half_ff, 128), half_ff)
        for b in range(2):
            right = cf[2 * j + b].reshape(1024, fc)
            store_dn(
                b, lax.dot_general(hidden[:, units], right, TN, preferred_element_type=F32)
            )

    def gg_out(j):
        rows = pl.ds(pl.multiple_of(j * fc, fc), fc)
        return pltpu.make_async_copy(acc.at[rows, 0:ff], gg_hbm.at[0, rows, :], o_sem.at[0, j])

    def ug_out(j):
        rows = pl.ds(pl.multiple_of(j * fc, fc), fc)
        return pltpu.make_async_copy(acc.at[rows, ff : 2 * ff], ug_hbm.at[0, rows, :], o_sem.at[1, j])

    def dg_out(j):
        cols = pl.ds(pl.multiple_of(j * 2 * fc, 2 * fc), 2 * fc)
        return pltpu.make_async_copy(dstage.at[lax.rem(j, 2)], dg_hbm.at[0, :, cols], o_sem.at[2, j])

    def back(c):
        feats = pl.ds(pl.multiple_of(c * fc, fc), fc)

        @pl.loop(0, SIDE)
        def _(s):
            rows = pl.ds(pl.multiple_of(s * 256, 256), 256)
            value = lax.dot_general(
                gcot[rows, :], wg[feats, :], NT, preferred_element_type=F32
            ) + lax.dot_general(ucot[rows, :], wu[feats, :], NT, preferred_element_type=F32)
            bq[c, s] = value.astype(BF).reshape(SIDE, SIDE, ROWS, fc)

    def ret_0(k, par):
        back(k)
        for j in (1, 3, 2):
            r_first(k, j).start()
        back(HC + k)
        start(t_first, k, par)

    def give_grads(j, par):
        @pl.when(j >= 2)
        def _():
            gu_send(j - 2).wait_send()
            dn_send(j - 2).wait_send()

        def store_gu(which, value):
            pgu[lax.rem(j, 2), :, which * ff : (which + 1) * ff] = value.astype(BF)

        def store_dn(b, value):
            pdn[lax.rem(j, 2), :, b * fc : (b + 1) * fc] = value.astype(BF)

        grads(j, other, store_gu, store_dn)
        gu_send(j).start()
        dn_send(j).start()

    def keep_grads(j, par):
        gu_send(j).wait_recv()
        dn_send(j).wait_recv()

        @pl.when(j >= 2)
        def _():
            dg_out(j - 2).wait()

        rows = pl.ds(pl.multiple_of(j * fc, fc), fc)

        def store_gu(which, value):
            cols = slice(which * ff, (which + 1) * ff)
            acc[rows, cols] = value + qgu[j, :, cols].astype(F32)

        def store_dn(b, value):
            cols = slice(b * fc, (b + 1) * fc)
            dstage[lax.rem(j, 2), :, cols] = value + qdn[j, :, cols].astype(F32)

        grads(j, d, store_gu, store_dn)
        gg_out(j).start()
        ug_out(j).start()
        dg_out(j).start()

    def ret_1(k, par):
        for j in (1, 3, 2):
            r_first(k, j).wait_recv()
        b1[k, :, :, own_half] = bq[k, z] + rz[k, 1]
        b1[k, :, :, far_half] = rz[k, 0] + rz[k, 2]
        start(r_second, k, par)
        arrive(t_first, k, par)
        start(t_second, k, par)

    def ret_2(k, par):
        arrive(r_second, k, par)
        start(r_third, k, par)
        arrive(t_second, k, par)
        for s in range(SIDE):
            ag[k, s] = lax.dot_general(
                sel1[s], t2[k, s].reshape(256, fc), TN, preferred_element_type=F32
            ).astype(BF)
        for j in (1, 3, 2):
            t_third(k, j).start()

    def ret_3(k, par):
        arrive(r_third, k, par)
        tokv[k] = lax.dot_general(
            sel2[...], rx[k].reshape(512, fc), TN, preferred_element_type=F32
        ).astype(BF)
        tok_out(k).start()
        for j in (1, 3, 2):
            t_third(k, j).wait_recv()
        total = ag[k, z].astype(F32)
        for j in range(3):
            total = total + pr[k, j].astype(F32)
        tokv[HC + k] = total.astype(BF)
        tok_out(HC + k).start()

    @pl.loop(0, HC)
    def _(i):
        for par in range(2):
            it = 2 * i + par
            for lag, work in (
                (0, ret_0),
                (0, give_grads),
                (1, ret_1),
                (4, keep_grads),
                (2, ret_2),
                (3, ret_3),
            ):

                @pl.when((it >= lag) & (it < HC + lag))
                def _():
                    work(it - lag, (par + lag) % 2)

    @pl.loop(0, HC // 2)
    def _(i):
        for par in range(2):
            k = 2 * i + par
            for hop in (r_second, r_third, t_first, t_second):
                sent(hop, k, par)
            for j in (1, 3, 2):
                r_first(k, j).wait_send()
                t_third(k, j).wait_send()

    for j in (HC - 2, HC - 1):
        gu_send(j).wait_send()
        dn_send(j).wait_send()
        dg_out(j).wait()
    for j in range(HC):
        gg_out(j).wait()
        ug_out(j).wait()
    for c in range(NC):
        tok_out(c).wait()


def hand_on(*refs):
    half = len(refs) // 2
    for src, dst in zip(refs[:half], refs[half:]):
        dst[...] = src[...]


def local(tokens, cotangent, experts, mixing, gate_matrix, up_matrix, down_matrix):
    width = tokens.shape[1]
    ff = gate_matrix.shape[2]
    fc = width // NC
    anywhere = pl.BlockSpec(memory_space=pl.ANY)
    in_vmem = pl.BlockSpec(memory_space=pltpu.VMEM)
    pair_rows = (SIDE, SIDE, 2, ROWS, fc)
    all_rows = (SIDE, SIDE, SIDE, ROWS, fc)
    shapes = (
        jax.ShapeDtypeStruct((TOK, width), BF),
        jax.ShapeDtypeStruct((1, width // 2, ff), F32),
        jax.ShapeDtypeStruct((1, width // 2, ff), F32),
        jax.ShapeDtypeStruct((1, ff // 2, width), F32),
    )
    results = pl.pallas_call(
        kernel,
        out_shape=shapes,
        in_specs=[in_vmem] * 2 + [anywhere] * 5,
        out_specs=(anywhere,) * 4,
        scratch_shapes=[
            pltpu.VMEM((NC, TOK, fc), BF),
            pltpu.VMEM((SIDE, 8, TOK), F32),
            pltpu.VMEM((512, TOK), BF),
            pltpu.VMEM((SIDE, 256, TOK), BF),
            pltpu.VMEM((SIDE, 256, 1), F32),
            pltpu.VMEM((NC,) + pair_rows, BF),
            pltpu.VMEM((NC,) + pair_rows, BF),
            pltpu.VMEM((NC,) + pair_rows, BF),
            pltpu.VMEM((NC,) + all_rows, BF),
            pltpu.VMEM((NC, SIDE, TOK, fc), BF),
            pltpu.VMEM((SLOTS,) + all_rows, BF),
            pltpu.VMEM((NC,) + all_rows, BF),
            pltpu.VMEM((NC,) + all_rows, BF),
            pltpu.VMEM((width, ff), BF),
            pltpu.VMEM((width, ff), BF),
            pltpu.VMEM((ff, width), BF),
            pltpu.VMEM((1024, 2 * ff), F32),
            pltpu.VMEM((1024, ff), F32),
            pltpu.VMEM((1024, ff), BF),
            pltpu.VMEM((1024, ff), BF),
            pltpu.VMEM((1024, ff), BF),
            pltpu.VMEM((HC, 3, SIDE, SIDE, ROWS, fc), BF),
            pltpu.VMEM((HC,) + pair_rows, BF),
            pltpu.VMEM((HC,) + pair_rows, BF),
            pltpu.VMEM((HC,) + all_rows, BF),
            pltpu.VMEM((HC,) + all_rows, BF),
            pltpu.VMEM((HC, 3, TOK, fc), BF),
            pltpu.VMEM((2, fc, 2 * ff), BF),
            pltpu.VMEM((2, ff // 2, 2 * fc), BF),
            pltpu.VMEM((HC, fc, 2 * ff), BF),
            pltpu.VMEM((HC, ff // 2, 2 * fc), BF),
            pltpu.VMEM((2, ff // 2, 2 * fc), F32),
            pltpu.SemaphoreType.DMA((2, NC)),
            pltpu.SemaphoreType.DMA((3,)),
            pltpu.SemaphoreType.DMA((10, NC)),
            pltpu.SemaphoreType.DMA((3,)),
            pltpu.SemaphoreType.DMA((3,)),
            pltpu.SemaphoreType.DMA((12, NC, 3)),
            pltpu.SemaphoreType.DMA((12, NC, 3)),
            pltpu.SemaphoreType.DMA((2, HC)),
            pltpu.SemaphoreType.DMA((2, HC)),
            pltpu.SemaphoreType.DMA((3, HC)),
        ],
        compiler_params=pltpu.CompilerParams(
            collective_id=0, has_side_effects=True, vmem_limit_bytes=67043328
        ),
    )(experts.T, mixing.T, tokens, cotangent, gate_matrix, up_matrix, down_matrix)
    steps = 8
    specs = [
        pl.BlockSpec((TOK // steps, width), lambda i: (i, 0)),
        pl.BlockSpec((1, width // 2 // steps, ff), lambda i: (0, i, 0)),
        pl.BlockSpec((1, width // 2 // steps, ff), lambda i: (0, i, 0)),
        pl.BlockSpec((1, ff // 2 // steps, width), lambda i: (0, i, 0)),
    ]
    return pl.pallas_call(
        hand_on, out_shape=shapes, grid=(steps,), in_specs=specs, out_specs=specs
    )(*results)


def solution(mesh):
    return jax.shard_map(
        local,
        mesh=mesh,
        in_specs=(
            P(("dp", "expert"), None),
            P(("dp", "expert"), None),
            P(("dp", "expert"), None),
            P(("dp", "expert"), None),
            P("expert", None, None),
            P("expert", None, None),
            P("expert", None, None),
        ),
        out_specs=(
            P(("dp", "expert"), None),
            P("expert", "dp", None),
            P("expert", "dp", None),
            P("expert", "dp", None),
        ),
        check_vma=False,
    )
```

```python
import jax
import jax.numpy as jnp
from jax import lax
from jax.experimental import pallas as pl
from jax.experimental.pallas import tpu as pltpu
from jax.sharding import PartitionSpec as P

MESH = pl.DeviceIdType.MESH
BF = jnp.bfloat16
F32 = jnp.float32
SIDE = 4
ROWS = 16
NC = 8
HC = NC // 2
SLOTS = 3
LAG1 = 2
LAG2 = 3
TOK = 128
NT = (((1,), (1,)), ((), ()))
TN = (((0,), (0,)), ((), ()))


def ranks(meta):
    pair_label = lax.broadcasted_iota(jnp.int32, (32, TOK), 0).astype(F32)
    onehots, names = [], []
    for k in range(4):
        name = meta[k : k + 1, :]
        names.append(name)
        pair = jnp.where(name >= 32.0, name - 32.0, name)
        onehots.append((pair_label == pair).astype(F32))
    count = onehots[0] + onehots[1] + onehots[2] + onehots[3]
    before = (
        lax.broadcasted_iota(jnp.int32, (TOK, TOK), 0)
        < lax.broadcasted_iota(jnp.int32, (TOK, TOK), 1)
    ).astype(BF)
    seen = jnp.dot(count.astype(BF), before, preferred_element_type=F32)
    out = []
    for k in range(4):
        out.append(jnp.sum(onehots[k] * seen, axis=0, keepdims=True))
        seen = seen + onehots[k]
    return names, out


def kernel(
    ids_ref,
    mix_ref,
    tok_hbm,
    cot_hbm,
    wg_hbm,
    wu_hbm,
    wd_hbm,
    out_ref,
    gg_ref,
    ug_ref,
    dg_ref,
    tokv,
    meta_z,
    sel2,
    sel1,
    mix1,
    x2,
    b1,
    b2,
    xf,
    ag,
    dq,
    bq,
    cf,
    wg,
    wu,
    wd,
    gcot,
    ucot,
    hidden,
    rz,
    ry,
    rx,
    t1,
    t2,
    pr,
    pgu,
    pdn,
    qgu,
    qdn,
    in_sem,
    w_sem,
    loc_sem,
    m_s,
    m_r,
    snd,
    rcv,
    p_s,
    p_r,
):
    fc = tokv.shape[2]
    ff = gcot.shape[1]
    half_ff = ff // 2
    d = lax.axis_index("dp")
    e = lax.axis_index("expert")
    z = lax.div(e, 16)
    y = lax.rem(lax.div(e, 4), 4)
    x = lax.rem(e, 4)
    other = 1 - d

    def at_z(v):
        return (d, v * 16 + y * 4 + x)

    def at_y(v):
        return (d, z * 16 + v * 4 + x)

    def at_x(v):
        return (d, z * 16 + y * 4 + v)

    def step(v, j):
        return lax.rem(v + j, SIDE)

    def slot(c):
        return lax.rem(c, SLOTS)

    def remote(src, dst, ssem, rsem, dev):
        return pltpu.make_async_remote_copy(
            src_ref=src, dst_ref=dst, send_sem=ssem, recv_sem=rsem, device_id=dev, device_id_type=MESH
        )

    def x_first(c, par):
        if par == 0:
            return x, at_x, lambda v: x2.at[c, v], b1.at[c, x]
        return y, at_y, lambda v: x2.at[c, :, v], b1.at[c, y]

    def x_second(c, par):
        if par == 0:
            return y, at_y, lambda v: b1.at[c, :, v], b2.at[c, y]
        return x, at_x, lambda v: b1.at[c, :, v], b2.at[c, :, x]

    def x_third(c, par):
        return z, at_z, lambda v: b2.at[c, :, :, lax.rem(v, 2)], xf.at[c, z]

    def c_first(c, par):
        return z, at_z, lambda v: ag.at[c, z], ag.at[c, z]

    def c_second(c, par):
        if par == 0:
            return y, at_y, lambda v: dq.at[slot(c), v], bq.at[c, :, y]
        return x, at_x, lambda v: dq.at[slot(c), v], bq.at[c, :, x]

    def c_third(c, par):
        if par == 0:
            return x, at_x, lambda v: bq.at[c, :, :, v], cf.at[c, :, :, x]
        return y, at_y, lambda v: bq.at[c, :, :, v], cf.at[c, :, y]

    def r_second(k, par):
        if par == 0:
            return y, at_y, lambda v: b1.at[k, v], ry.at[k, y]
        return x, at_x, lambda v: b1.at[k, :, v], ry.at[k, x]

    def r_third(k, par):
        if par == 0:
            return x, at_x, lambda v: ry.at[k, :, v], rx.at[k, x]
        return y, at_y, lambda v: ry.at[k, :, v], rx.at[k, :, y]

    def t_first(k, par):
        if par == 0:
            return x, at_x, lambda v: bq.at[HC + k, :, :, v], t1.at[k, :, x]
        return y, at_y, lambda v: bq.at[HC + k, :, v], t1.at[k, :, y]

    def t_second(k, par):
        if par == 0:
            return y, at_y, lambda v: t1.at[k, :, :, v], t2.at[k, :, y]
        return x, at_x, lambda v: t1.at[k, :, :, v], t2.at[k, :, :, x]

    hops = [x_first, x_second, x_third, c_first, c_second, c_third, r_second, r_third, t_first, t_second]

    def copy_of(hop, c, par, j):
        i = hops.index(hop)
        here, at, src, dst = hop(c, par)
        v = step(here, j)
        return remote(src(v), dst, snd.at[i, c, j - 1], rcv.at[i, c, j - 1], at(v))

    def own_copy(hop, c, par):
        here, _, src, dst = hop(c, par)
        return pltpu.make_async_copy(src(here), dst, loc_sem.at[hops.index(hop), c])

    def start(hop, c, par):
        for j in (1, 3, 2):
            copy_of(hop, c, par, j).start()
        if hop is not c_first:
            own_copy(hop, c, par).start()

    def arrive(hop, c, par):
        for j in (1, 3, 2):
            copy_of(hop, c, par, j).wait_recv()
        if hop is not c_first:
            own_copy(hop, c, par).wait()

    def sent(hop, c, par):
        for j in (1, 3, 2):
            copy_of(hop, c, par, j).wait_send()

    def r_first(k, j):
        v = step(z, j)
        i = len(hops)
        return remote(bq.at[k, v], rz.at[k, j - 1], snd.at[i, k, j - 1], rcv.at[i, k, j - 1], at_z(v))

    def t_third(k, j):
        v = step(z, j)
        i = len(hops) + 1
        return remote(ag.at[k, v], pr.at[k, j - 1], snd.at[i, k, j - 1], rcv.at[i, k, j - 1], at_z(v))

    def mz(j):
        return remote(meta_z.at[z], meta_z.at[z], m_s.at[j - 1], m_r.at[j - 1], at_z(step(z, j)))

    def tok_in(c):
        cols = pl.ds(pl.multiple_of(c * fc, fc), fc)
        return pltpu.make_async_copy(tok_hbm.at[:, cols], tokv.at[c], in_sem.at[0, c])

    def cot_in(c):
        cols = pl.ds(pl.multiple_of(c * fc, fc), fc)
        return pltpu.make_async_copy(cot_hbm.at[:, cols], ag.at[c, z], in_sem.at[1, c])

    weights_in = [
        pltpu.make_async_copy(wg_hbm.at[0], wg, w_sem.at[0]),
        pltpu.make_async_copy(wu_hbm.at[0], wu, w_sem.at[1]),
        pltpu.make_async_copy(wd_hbm.at[0], wd, w_sem.at[2]),
    ]

    @pl.loop(0, NC)
    def _(c):
        cot_in(c).start()
        tok_in(c).start()

    for copy in weights_in:
        copy.start()

    barrier = pltpu.get_barrier_semaphore()
    for j in (1, 2, 3):
        for dev in (at_x(step(x, j)), at_y(step(y, j)), at_z(step(z, j))):
            pl.semaphore_signal(barrier, inc=1, device_id=dev, device_id_type=MESH)
    pl.semaphore_signal(barrier, inc=1, device_id=(other, e), device_id_type=MESH)

    meta_z[z, 0:4, :] = ids_ref[...].astype(F32)
    meta_z[z, 4:8, :] = mix_ref[...]
    names, rank = ranks(ids_ref[...].astype(F32))
    slots = []
    for k in range(4):
        pair = jnp.where(names[k] >= 32.0, names[k] - 32.0, names[k])
        high = (pair >= 16.0).astype(F32)
        rest = pair - 16.0 * high
        row = jnp.floor(rest * 0.25)
        slots.append(((rest - 4.0 * row) * 8.0 + row * 2.0 + high) * ROWS + rank[k])
    slot_label = lax.broadcasted_iota(jnp.int32, (512, TOK), 0).astype(F32)
    picked = (slot_label == slots[0]).astype(F32)
    for k in range(1, 4):
        picked = picked + (slot_label == slots[k]).astype(F32)
    sel2[...] = picked.astype(BF)

    pl.semaphore_wait(barrier, 10)
    for j in (1, 3, 2):
        mz(j).start()

    @pl.loop(0, HC)
    def _(i):
        for par in range(2):
            c = 2 * i + par
            cot_in(c).wait()
            start(c_first, c, par)
            tok_in(c).wait()
            rows = jnp.dot(sel2[...], tokv[c], preferred_element_type=F32).astype(BF)
            x2[c] = rows.reshape(SIDE, SIDE, 2, ROWS, fc)
            start(x_first, c, par)

    for j in (1, 3, 2):
        mz(j).wait_recv()
    plane = z.astype(F32) * 16.0
    label1 = lax.broadcasted_iota(jnp.int32, (256, TOK), 0).astype(F32)
    for s in range(SIDE):
        names_s, rank_s = ranks(meta_z[s])
        picked = jnp.zeros((256, TOK), F32)
        mixed = jnp.zeros((256, TOK), F32)
        for k in range(4):
            hit = label1 == (names_s[k] - plane) * ROWS + rank_s[k]
            picked = picked + hit.astype(F32)
            mixed = mixed + jnp.where(hit, meta_z[s, 4 + k : 5 + k, :], 0.0)
        sel1[s] = picked.astype(BF)
        mix1[s] = jnp.sum(mixed, axis=1, keepdims=True)

    for ref in (gg_ref, ug_ref, dg_ref):
        ref[...] = jnp.zeros_like(ref)
    for copy in weights_in:
        copy.wait()

    def second_hops(c, par):
        arrive(x_first, c, par)
        start(x_second, c, par)
        arrive(c_first, c, par)

        @pl.when(c >= SLOTS)
        def _():
            sent(c_second, c - SLOTS, (par + SLOTS) % 2)

        for s in range(SIDE):
            rows = jnp.dot(sel1[s], ag[c, s], preferred_element_type=F32) * mix1[s]
            rows = rows.astype(BF).reshape(SIDE, SIDE, ROWS, fc)
            if par == 0:
                dq[slot(c), :, s] = rows
            else:
                for v in range(SIDE):
                    dq[slot(c), :, s, v] = rows[v]
        start(c_second, c, par)

    def third_hops(c, par):
        arrive(x_second, c, par)
        start(x_third, c, par)
        arrive(c_second, c, par)
        start(c_third, c, par)

    def multiply(c, par):
        feats = pl.ds(pl.multiple_of(c * fc, fc), fc)
        arrive(x_third, c, par)
        block = xf[c].reshape(1024, fc)
        for n in range(0, ff, 256):
            units = slice(n, n + 256)
            gg_ref[0, :, units] += jnp.dot(block, wg[feats, units], preferred_element_type=F32)
            ug_ref[0, :, units] += jnp.dot(block, wu[feats, units], preferred_element_type=F32)
        arrive(c_third, c, par)
        block = cf[c].reshape(1024, fc)
        for u in range(ff // 256):
            value = lax.dot_general(
                block, wd[u * 256 : (u + 1) * 256, feats], NT, preferred_element_type=F32
            )
            for r in range(8):
                dg_ref[0, u * 128 : (u + 1) * 128, r * 256 : (r + 1) * 256] += value[
                    r * 128 : (r + 1) * 128
                ]

    @pl.loop(0, HC + 2)
    def _(i):
        for par in range(2):
            it = 2 * i + par
            for lag, work in ((0, second_hops), (LAG1, third_hops), (LAG2, multiply)):

                @pl.when((it >= lag) & (it < NC + lag))
                def _():
                    work(it - lag, (par + lag) % 2)

    @pl.loop(0, 16)
    def _(i):
        rows = pl.ds(pl.multiple_of(i * 64, 64), 64)
        place = pl.multiple_of(lax.div(i, 2) * 256, 256)
        part = pl.multiple_of(lax.rem(i, 2) * 64, 64)
        for u in range(ff // 256):
            units = slice(u * 256, (u + 1) * 256)
            pre_gate = gg_ref[0, rows, units]
            pre_up = ug_ref[0, rows, units]
            hidden_cot = dg_ref[0, pl.ds(u * 128 + part, 64), pl.ds(place, 256)]
            sigmoid_gate = jax.nn.sigmoid(pre_gate)
            activated = pre_gate * sigmoid_gate
            hidden[rows, units] = (activated * pre_up).astype(BF)
            gcot[rows, units] = (
                hidden_cot * pre_up * sigmoid_gate * (1.0 + pre_gate * (1.0 - sigmoid_gate))
            ).astype(BF)
            ucot[rows, units] = (hidden_cot * activated).astype(BF)

    @pl.loop(0, HC)
    def _(i):
        for par in range(2):
            c = 2 * i + par
            for hop in (x_first, x_second, x_third, c_first, c_third):
                sent(hop, c, par)

    for c in range(NC - SLOTS, NC):
        sent(c_second, c, c % 2)
    for j in (1, 3, 2):
        mz(j).wait_send()

    own_half = lax.rem(z, 2)
    far_half = 1 - own_half

    def gu_send(j):
        return remote(pgu.at[lax.rem(j, 2)], qgu.at[j], p_s.at[0, j], p_r.at[0, j], (other, e))

    def dn_send(j):
        return remote(pdn.at[lax.rem(j, 2)], qdn.at[j], p_s.at[1, j], p_r.at[1, j], (other, e))

    def grads(j, side, store_gu, store_dn):
        c = side * HC + j
        left = xf[c].reshape(1024, fc)
        store_gu(0, lax.dot_general(left, gcot[...], TN, preferred_element_type=F32))
        store_gu(1, lax.dot_general(left, ucot[...], TN, preferred_element_type=F32))
        units = pl.ds(pl.multiple_of(side * half_ff, 128), half_ff)
        for b in range(2):
            right = cf[2 * j + b].reshape(1024, fc)
            store_dn(
                b, lax.dot_general(hidden[:, units], right, TN, preferred_element_type=F32)
            )

    def back(c):
        feats = pl.ds(pl.multiple_of(c * fc, fc), fc)
        value = lax.dot_general(
            gcot[...], wg[feats, :], NT, preferred_element_type=F32
        ) + lax.dot_general(ucot[...], wu[feats, :], NT, preferred_element_type=F32)
        bq[c] = value.astype(BF).reshape(SIDE, SIDE, SIDE, ROWS, fc)

    def ret_0(k, par):
        back(k)
        for j in (1, 3, 2):
            r_first(k, j).start()
        back(HC + k)
        start(t_first, k, par)

    def give_grads(j, par):
        @pl.when(j >= 2)
        def _():
            gu_send(j - 2).wait_send()
            dn_send(j - 2).wait_send()

        def store_gu(which, value):
            pgu[lax.rem(j, 2), :, which * ff : (which + 1) * ff] = value.astype(BF)

        def store_dn(b, value):
            pdn[lax.rem(j, 2), :, b * fc : (b + 1) * fc] = value.astype(BF)

        grads(j, other, store_gu, store_dn)
        gu_send(j).start()
        dn_send(j).start()

    def keep_grads(j, par):
        gu_send(j).wait_recv()
        dn_send(j).wait_recv()

        rows = pl.ds(pl.multiple_of(j * fc, fc), fc)

        def store_gu(which, value):
            ref = (gg_ref, ug_ref)[which]
            ref[0, rows, :] = value + qgu[j, :, which * ff : (which + 1) * ff].astype(F32)

        def store_dn(b, value):
            cols = pl.ds(pl.multiple_of((2 * j + b) * fc, fc), fc)
            dg_ref[0, :, cols] = value + qdn[j, :, b * fc : (b + 1) * fc].astype(F32)

        grads(j, d, store_gu, store_dn)

    def ret_1(k, par):
        for j in (1, 3, 2):
            r_first(k, j).wait_recv()
        b1[k, :, :, own_half] = bq[k, z] + rz[k, 1]
        b1[k, :, :, far_half] = rz[k, 0] + rz[k, 2]
        start(r_second, k, par)
        arrive(t_first, k, par)
        start(t_second, k, par)

    def ret_2(k, par):
        arrive(r_second, k, par)
        start(r_third, k, par)
        arrive(t_second, k, par)
        for s in range(SIDE):
            ag[k, s] = lax.dot_general(
                sel1[s], t2[k, s].reshape(256, fc), TN, preferred_element_type=F32
            ).astype(BF)
        for j in (1, 3, 2):
            t_third(k, j).start()

    def ret_3(k, par):
        arrive(r_third, k, par)
        cols = pl.ds(pl.multiple_of(k * fc, fc), fc)
        out_ref[:, cols] = lax.dot_general(
            sel2[...], rx[k].reshape(512, fc), TN, preferred_element_type=F32
        ).astype(BF)
        for j in (1, 3, 2):
            t_third(k, j).wait_recv()
        total = ag[k, z].astype(F32)
        for j in range(3):
            total = total + pr[k, j].astype(F32)
        cols = pl.ds(pl.multiple_of((HC + k) * fc, fc), fc)
        out_ref[:, cols] = total.astype(BF)

    @pl.loop(0, HC)
    def _(i):
        for par in range(2):
            it = 2 * i + par
            for lag, work in (
                (0, ret_0),
                (2, ret_1),
                (2, give_grads),
                (3, ret_2),
                (4, keep_grads),
                (4, ret_3),
            ):

                @pl.when((it >= lag) & (it < HC + lag))
                def _():
                    work(it - lag, (par + lag) % 2)

    @pl.loop(0, HC // 2)
    def _(i):
        for par in range(2):
            k = 2 * i + par
            for hop in (r_second, r_third, t_first, t_second):
                sent(hop, k, par)
            for j in (1, 3, 2):
                r_first(k, j).wait_send()
                t_third(k, j).wait_send()

    for j in (HC - 2, HC - 1):
        gu_send(j).wait_send()
        dn_send(j).wait_send()


PIECES = 4


def hand_on(*refs):
    sem = refs[8]
    copies = []
    for i in range(4):
        src, dst = refs[i], refs[4 + i]
        if i > 0:
            src, dst = src.at[0], dst.at[0]
        part = src.shape[0] // PIECES
        for n in range(PIECES):
            rows = pl.ds(n * part, part)
            copies.append(pltpu.make_async_copy(src.at[rows], dst.at[rows], sem.at[i, n]))
    for copy in copies:
        copy.start()
    for copy in copies:
        copy.wait()


def local(tokens, cotangent, experts, mixing, gate_matrix, up_matrix, down_matrix):
    width = tokens.shape[1]
    ff = gate_matrix.shape[2]
    fc = width // NC
    anywhere = pl.BlockSpec(memory_space=pl.ANY)
    in_vmem = pl.BlockSpec(memory_space=pltpu.VMEM)
    pair_rows = (SIDE, SIDE, 2, ROWS, fc)
    all_rows = (SIDE, SIDE, SIDE, ROWS, fc)
    shapes = (
        jax.ShapeDtypeStruct((TOK, width), BF),
        jax.ShapeDtypeStruct((1, width // 2, ff), F32),
        jax.ShapeDtypeStruct((1, width // 2, ff), F32),
        jax.ShapeDtypeStruct((1, ff // 2, width), F32),
    )
    results = pl.pallas_call(
        kernel,
        out_shape=tuple(pltpu.VMEM(s.shape, s.dtype) for s in shapes),
        in_specs=[in_vmem] * 2 + [anywhere] * 5,
        out_specs=(in_vmem,) * 4,
        scratch_shapes=[
            pltpu.VMEM((NC, TOK, fc), BF),
            pltpu.VMEM((SIDE, 8, TOK), F32),
            pltpu.VMEM((512, TOK), BF),
            pltpu.VMEM((SIDE, 256, TOK), BF),
            pltpu.VMEM((SIDE, 256, 1), F32),
            pltpu.VMEM((NC,) + pair_rows, BF),
            pltpu.VMEM((NC,) + pair_rows, BF),
            pltpu.VMEM((NC,) + pair_rows, BF),
            pltpu.VMEM((NC,) + all_rows, BF),
            pltpu.VMEM((NC, SIDE, TOK, fc), BF),
            pltpu.VMEM((SLOTS,) + all_rows, BF),
            pltpu.VMEM((NC,) + all_rows, BF),
            pltpu.VMEM((NC,) + all_rows, BF),
            pltpu.VMEM((width, ff), BF),
            pltpu.VMEM((width, ff), BF),
            pltpu.VMEM((ff, width), BF),
            pltpu.VMEM((1024, ff), BF),
            pltpu.VMEM((1024, ff), BF),
            pltpu.VMEM((1024, ff), BF),
            pltpu.VMEM((HC, 3, SIDE, SIDE, ROWS, fc), BF),
            pltpu.VMEM((HC,) + pair_rows, BF),
            pltpu.VMEM((HC,) + pair_rows, BF),
            pltpu.VMEM((HC,) + all_rows, BF),
            pltpu.VMEM((HC,) + all_rows, BF),
            pltpu.VMEM((HC, 3, TOK, fc), BF),
            pltpu.VMEM((2, fc, 2 * ff), BF),
            pltpu.VMEM((2, ff // 2, 2 * fc), BF),
            pltpu.VMEM((HC, fc, 2 * ff), BF),
            pltpu.VMEM((HC, ff // 2, 2 * fc), BF),
            pltpu.SemaphoreType.DMA((2, NC)),
            pltpu.SemaphoreType.DMA((3,)),
            pltpu.SemaphoreType.DMA((10, NC)),
            pltpu.SemaphoreType.DMA((3,)),
            pltpu.SemaphoreType.DMA((3,)),
            pltpu.SemaphoreType.DMA((12, NC, 3)),
            pltpu.SemaphoreType.DMA((12, NC, 3)),
            pltpu.SemaphoreType.DMA((2, HC)),
            pltpu.SemaphoreType.DMA((2, HC)),
        ],
        compiler_params=pltpu.CompilerParams(
            collective_id=0, has_side_effects=True, vmem_limit_bytes=56500000
        ),
    )(experts.T, mixing.T, tokens, cotangent, gate_matrix, up_matrix, down_matrix)
    return pl.pallas_call(
        hand_on,
        out_shape=shapes,
        in_specs=[in_vmem] * 4,
        out_specs=(anywhere,) * 4,
        scratch_shapes=[pltpu.SemaphoreType.DMA((4, PIECES))],
        compiler_params=pltpu.CompilerParams(vmem_limit_bytes=1 << 20),
    )(*(pltpu.with_memory_space_constraint(value, pltpu.VMEM) for value in results))


def solution(mesh):
    return jax.shard_map(
        local,
        mesh=mesh,
        in_specs=(
            P(("dp", "expert"), None),
            P(("dp", "expert"), None),
            P(("dp", "expert"), None),
            P(("dp", "expert"), None),
            P("expert", None, None),
            P("expert", None, None),
            P("expert", None, None),
        ),
        out_specs=(
            P(("dp", "expert"), None),
            P("expert", "dp", None),
            P("expert", "dp", None),
            P("expert", "dp", None),
        ),
        check_vma=False,
    )
```

```python
import jax
import jax.numpy as jnp
from jax import lax
from jax.experimental import pallas as pl
from jax.experimental.pallas import tpu as pltpu
from jax.sharding import PartitionSpec as P

MESH = pl.DeviceIdType.MESH
BF = jnp.bfloat16
F32 = jnp.float32
SIDE = 4
ROWS = 16
NC = 8
HC = NC // 2
SLOTS = 3
LAG1 = 2
AHEAD = 3
LAG2 = 3
TOK = 128
NT = (((1,), (1,)), ((), ()))
TN = (((0,), (0,)), ((), ()))


def ranks(meta):
    pair_label = lax.broadcasted_iota(jnp.int32, (32, TOK), 0).astype(F32)
    onehots, names = [], []
    for k in range(4):
        name = meta[k : k + 1, :]
        names.append(name)
        pair = jnp.where(name >= 32.0, name - 32.0, name)
        onehots.append((pair_label == pair).astype(F32))
    count = onehots[0] + onehots[1] + onehots[2] + onehots[3]
    before = (
        lax.broadcasted_iota(jnp.int32, (TOK, TOK), 0)
        < lax.broadcasted_iota(jnp.int32, (TOK, TOK), 1)
    ).astype(BF)
    seen = jnp.dot(count.astype(BF), before, preferred_element_type=F32)
    out = []
    for k in range(4):
        out.append(jnp.sum(onehots[k] * seen, axis=0, keepdims=True))
        seen = seen + onehots[k]
    return names, out


def kernel(
    ids_ref,
    mix_ref,
    tok_hbm,
    cot_hbm,
    wg_hbm,
    wu_hbm,
    wd_hbm,
    out_ref,
    gg_ref,
    ug_ref,
    dg_ref,
    tokv,
    meta_z,
    sel2,
    sel1,
    mix1,
    x2,
    b1,
    b2,
    xf,
    ag,
    dq,
    bq,
    cf,
    wg,
    wu,
    wd,
    gcot,
    ucot,
    hidden,
    rz,
    ry,
    rx,
    t1,
    t2,
    pr,
    pgu,
    pdn,
    qgu,
    qdn,
    in_sem,
    w_sem,
    m_sem,
    snd,
    rcv,
    p_s,
    p_r,
):
    fc = tokv.shape[2]
    ff = gcot.shape[1]
    half_ff = ff // 2
    d = lax.axis_index("dp")
    e = lax.axis_index("expert")
    z = lax.div(e, 16)
    y = lax.rem(lax.div(e, 4), 4)
    x = lax.rem(e, 4)
    other = 1 - d

    def at_z(v):
        return (d, v * 16 + y * 4 + x)

    def at_y(v):
        return (d, z * 16 + v * 4 + x)

    def at_x(v):
        return (d, z * 16 + y * 4 + v)

    def step(v, j):
        return lax.rem(v + j, SIDE)

    def slot(c):
        return lax.rem(c, SLOTS)

    def remote(src, dst, ssem, rsem, dev):
        return pltpu.make_async_remote_copy(
            src_ref=src, dst_ref=dst, send_sem=ssem, recv_sem=rsem, device_id=dev, device_id_type=MESH
        )

    def x_first(c, par):
        if par == 0:
            return x, at_x, lambda v: x2.at[c, v], b1.at[c, x]
        return y, at_y, lambda v: x2.at[c, :, v], b1.at[c, y]

    def x_second(c, par):
        if par == 0:
            return y, at_y, lambda v: b1.at[c, :, v], b2.at[c, y]
        return x, at_x, lambda v: b1.at[c, :, v], b2.at[c, :, x]

    def x_third(c, par):
        return z, at_z, lambda v: b2.at[c, :, :, lax.rem(v, 2)], xf.at[c, z]

    def c_first(c, par):
        return z, at_z, lambda v: ag.at[c, z], ag.at[c, z]

    def c_second(c, par):
        if par == 0:
            return y, at_y, lambda v: dq.at[slot(c), v], bq.at[c, :, y]
        return x, at_x, lambda v: dq.at[slot(c), v], bq.at[c, :, x]

    def c_third(c, par):
        if par == 0:
            return x, at_x, lambda v: bq.at[c, :, :, v], cf.at[c, :, :, x]
        return y, at_y, lambda v: bq.at[c, :, :, v], cf.at[c, :, y]

    def r_second(k, par):
        if par == 0:
            return y, at_y, lambda v: b1.at[k, v], ry.at[k, y]
        return x, at_x, lambda v: b1.at[k, :, v], ry.at[k, x]

    def r_third(k, par):
        if par == 0:
            return x, at_x, lambda v: ry.at[k, :, v], rx.at[k, x]
        return y, at_y, lambda v: ry.at[k, :, v], rx.at[k, :, y]

    def t_first(k, par):
        if par == 0:
            return x, at_x, lambda v: bq.at[HC + k, :, :, v], t1.at[k, :, x]
        return y, at_y, lambda v: bq.at[HC + k, :, v], t1.at[k, :, y]

    def t_second(k, par):
        if par == 0:
            return y, at_y, lambda v: t1.at[k, :, :, v], t2.at[k, :, y]
        return x, at_x, lambda v: t1.at[k, :, :, v], t2.at[k, :, :, x]

    hops = [x_first, x_second, x_third, c_first, c_second, c_third, r_second, r_third, t_first, t_second]

    def landing(hop, c):
        i = hops.index(hop)
        return rcv.at[i * NC + c if i < 6 else 6 * NC + (i - 6) * HC + c]

    def leaving(hop, c):
        return snd.at[len(hops) + 2 + slot(c) if hop is c_second else hops.index(hop)]

    def wait_for(ref, sem):
        pltpu.make_async_copy(ref, ref, sem).wait()

    def start(hop, c, par):
        here, at, src, dst = hop(c, par)
        for j in (1, 3, 2):
            v = step(here, j)
            remote(src(v), dst, leaving(hop, c), landing(hop, c), at(v)).start()
        if hop is not c_first:
            pltpu.make_async_copy(src(here), dst, landing(hop, c)).start()

    def arrive(hop, c):
        ref = (b1, b2, xf, ag, bq, cf, ry, rx, t1, t2)[hops.index(hop)].at[c]
        wait_for(ref.at[0:3] if hop is c_first else ref, landing(hop, c))

    def r_first(k):
        for j in (1, 3, 2):
            v = step(z, j)
            sem = rcv.at[6 * NC + 4 * HC + k]
            remote(bq.at[k, v], rz.at[k, j - 1], snd.at[len(hops)], sem, at_z(v)).start()

    def t_third(k):
        for j in (1, 3, 2):
            v = step(z, j)
            sem = rcv.at[6 * NC + 5 * HC + k]
            remote(ag.at[k, v], pr.at[k, j - 1], snd.at[len(hops) + 1], sem, at_z(v)).start()

    def tok_in(c):
        cols = pl.ds(pl.multiple_of(c * fc, fc), fc)
        return pltpu.make_async_copy(tok_hbm.at[:, cols], tokv.at[c], in_sem.at[0])

    def cot_in(c):
        cols = pl.ds(pl.multiple_of(c * fc, fc), fc)
        return pltpu.make_async_copy(cot_hbm.at[:, cols], ag.at[c, z], in_sem.at[1])

    weights_in = [
        pltpu.make_async_copy(wg_hbm.at[0], wg, w_sem.at[0]),
        pltpu.make_async_copy(wu_hbm.at[0], wu, w_sem.at[1]),
        pltpu.make_async_copy(wd_hbm.at[0], wd, w_sem.at[2]),
    ]

    @pl.loop(0, NC)
    def _(c):
        cot_in(c).start()
        tok_in(c).start()

    barrier = pltpu.get_barrier_semaphore()
    for j in (1, 2, 3):
        for dev in (at_x(step(x, j)), at_y(step(y, j)), at_z(step(z, j))):
            pl.semaphore_signal(barrier, inc=1, device_id=dev, device_id_type=MESH)
    pl.semaphore_signal(barrier, inc=1, device_id=(other, e), device_id_type=MESH)

    meta_z[z, 0:4, :] = ids_ref[...].astype(F32)
    meta_z[z, 4:8, :] = mix_ref[...]
    names, rank = ranks(ids_ref[...].astype(F32))
    slots = []
    for k in range(4):
        pair = jnp.where(names[k] >= 32.0, names[k] - 32.0, names[k])
        high = (pair >= 16.0).astype(F32)
        rest = pair - 16.0 * high
        row = jnp.floor(rest * 0.25)
        slots.append(((rest - 4.0 * row) * 8.0 + row * 2.0 + high) * ROWS + rank[k])
    slot_label = lax.broadcasted_iota(jnp.int32, (512, TOK), 0).astype(F32)
    picked = (slot_label == slots[0]).astype(F32)
    for k in range(1, 4):
        picked = picked + (slot_label == slots[k]).astype(F32)
    sel2[...] = picked.astype(BF)
    wait_for(tokv, in_sem.at[1])
    wait_for(tokv, in_sem.at[0])
    for copy in weights_in:
        copy.start()

    pl.semaphore_wait(barrier, 10)
    for j in (1, 3, 2):
        v = step(z, j)
        remote(meta_z.at[z], meta_z.at[z], m_sem.at[0], m_sem.at[1], at_z(v)).start()

    def first_hops(c, par):
        start(c_first, c, par)
        rows = jnp.dot(sel2[...], tokv[c], preferred_element_type=F32).astype(BF)
        x2[c] = rows.reshape(SIDE, SIDE, 2, ROWS, fc)
        start(x_first, c, par)

    for c in range(AHEAD):
        first_hops(c, c % 2)
    wait_for(meta_z.at[0:3], m_sem.at[1])
    plane = z.astype(F32) * 16.0
    label1 = lax.broadcasted_iota(jnp.int32, (256, TOK), 0).astype(F32)
    for s in range(SIDE):
        names_s, rank_s = ranks(meta_z[s])
        picked = jnp.zeros((256, TOK), F32)
        mixed = jnp.zeros((256, TOK), F32)
        for k in range(4):
            hit = label1 == (names_s[k] - plane) * ROWS + rank_s[k]
            picked = picked + hit.astype(F32)
            mixed = mixed + jnp.where(hit, meta_z[s, 4 + k : 5 + k, :], 0.0)
        sel1[s] = picked.astype(BF)
        mix1[s] = jnp.sum(mixed, axis=1, keepdims=True)

    for ref in (gg_ref, ug_ref, dg_ref):
        ref[...] = jnp.zeros_like(ref)
    for copy in weights_in:
        copy.wait()

    def second_hops(c, par):
        arrive(x_first, c)
        start(x_second, c, par)
        arrive(c_first, c)

        @pl.when(c >= SLOTS)
        def _():
            wait_for(dq.at[slot(c), 0:3], leaving(c_second, c))

        for s in range(SIDE):
            rows = jnp.dot(sel1[s], ag[c, s], preferred_element_type=F32) * mix1[s]
            rows = rows.astype(BF).reshape(SIDE, SIDE, ROWS, fc)
            if par == 0:
                dq[slot(c), :, s] = rows
            else:
                for v in range(SIDE):
                    dq[slot(c), :, s, v] = rows[v]
        start(c_second, c, par)

        @pl.when(c + AHEAD < NC)
        def _():
            first_hops(c + AHEAD, (par + AHEAD) % 2)

    def third_hops(c, par):
        arrive(x_second, c)
        start(x_third, c, par)
        arrive(c_second, c)
        start(c_third, c, par)

    def multiply(c, par):
        feats = pl.ds(pl.multiple_of(c * fc, fc), fc)
        arrive(x_third, c)
        block = xf[c].reshape(1024, fc)
        for n in range(0, ff, 256):
            units = slice(n, n + 256)
            gg_ref[0, :, units] += jnp.dot(block, wg[feats, units], preferred_element_type=F32)
            ug_ref[0, :, units] += jnp.dot(block, wu[feats, units], preferred_element_type=F32)
        arrive(c_third, c)
        block = cf[c].reshape(1024, fc)
        for u in range(ff // 256):
            value = lax.dot_general(
                block, wd[u * 256 : (u + 1) * 256, feats], NT, preferred_element_type=F32
            )
            for r in range(8):
                dg_ref[0, u * 128 : (u + 1) * 128, r * 256 : (r + 1) * 256] += value[
                    r * 128 : (r + 1) * 128
                ]

    @pl.loop(0, HC + 2)
    def _(i):
        for par in range(2):
            it = 2 * i + par
            for lag, work in ((0, second_hops), (LAG1, third_hops), (LAG2, multiply)):

                @pl.when((it >= lag) & (it < NC + lag))
                def _():
                    work(it - lag, (par + lag) % 2)

    @pl.loop(0, 16)
    def _(i):
        rows = pl.ds(pl.multiple_of(i * 64, 64), 64)
        place = pl.multiple_of(lax.div(i, 2) * 256, 256)
        part = pl.multiple_of(lax.rem(i, 2) * 64, 64)
        for u in range(ff // 256):
            units = slice(u * 256, (u + 1) * 256)
            pre_gate = gg_ref[0, rows, units]
            pre_up = ug_ref[0, rows, units]
            hidden_cot = dg_ref[0, pl.ds(u * 128 + part, 64), pl.ds(place, 256)]
            sigmoid_gate = jax.nn.sigmoid(pre_gate)
            activated = pre_gate * sigmoid_gate
            hidden[rows, units] = (activated * pre_up).astype(BF)
            gcot[rows, units] = (
                hidden_cot * pre_up * sigmoid_gate * (1.0 + pre_gate * (1.0 - sigmoid_gate))
            ).astype(BF)
            ucot[rows, units] = (hidden_cot * activated).astype(BF)

    for hop, ref in (
        (x_first, x2.at[:, 0:3]),
        (x_second, b2.at[:, 0:3]),
        (x_third, xf.at[:, 0:3]),
        (c_first, ag.at[:, 0:3]),
        (c_third, cf.at[:, 0:3]),
    ):
        wait_for(ref, leaving(hop, 0))
    for c in range(NC - SLOTS, NC):
        wait_for(dq.at[slot(c), 0:3], leaving(c_second, c))
    wait_for(meta_z.at[0:3], m_sem.at[0])

    own_half = lax.rem(z, 2)
    far_half = 1 - own_half

    def gu_send(j):
        return remote(pgu.at[lax.rem(j, 2)], qgu.at[j], p_s.at[0, lax.rem(j, 2)], p_r.at[0, j], (other, e))

    def dn_send(j):
        return remote(pdn.at[lax.rem(j, 2)], qdn.at[j], p_s.at[1, lax.rem(j, 2)], p_r.at[1, j], (other, e))

    def grads(j, side, store_gu, store_dn):
        c = side * HC + j
        left = xf[c].reshape(1024, fc)
        store_gu(0, lax.dot_general(left, gcot[...], TN, preferred_element_type=F32))
        store_gu(1, lax.dot_general(left, ucot[...], TN, preferred_element_type=F32))
        units = pl.ds(pl.multiple_of(side * half_ff, 128), half_ff)
        for b in range(2):
            right = cf[2 * j + b].reshape(1024, fc)
            store_dn(
                b, lax.dot_general(hidden[:, units], right, TN, preferred_element_type=F32)
            )

    def back(c):
        feats = pl.ds(pl.multiple_of(c * fc, fc), fc)
        value = lax.dot_general(
            gcot[...], wg[feats, :], NT, preferred_element_type=F32
        ) + lax.dot_general(ucot[...], wu[feats, :], NT, preferred_element_type=F32)
        bq[c] = value.astype(BF).reshape(SIDE, SIDE, SIDE, ROWS, fc)

    def ret_0(k, par):
        back(k)
        r_first(k)
        back(HC + k)
        start(t_first, k, par)

    def give_grads(j, par):
        @pl.when(j >= 2)
        def _():
            gu_send(j - 2).wait_send()
            dn_send(j - 2).wait_send()

        def store_gu(which, value):
            pgu[lax.rem(j, 2), :, which * ff : (which + 1) * ff] = value.astype(BF)

        def store_dn(b, value):
            pdn[lax.rem(j, 2), :, b * fc : (b + 1) * fc] = value.astype(BF)

        grads(j, other, store_gu, store_dn)
        gu_send(j).start()
        dn_send(j).start()

    def keep_grads(j, par):
        gu_send(j).wait_recv()
        dn_send(j).wait_recv()

        rows = pl.ds(pl.multiple_of(j * fc, fc), fc)

        def store_gu(which, value):
            ref = (gg_ref, ug_ref)[which]
            ref[0, rows, :] = value + qgu[j, :, which * ff : (which + 1) * ff].astype(F32)

        def store_dn(b, value):
            cols = pl.ds(pl.multiple_of((2 * j + b) * fc, fc), fc)
            dg_ref[0, :, cols] = value + qdn[j, :, b * fc : (b + 1) * fc].astype(F32)

        grads(j, d, store_gu, store_dn)

    def ret_1(k, par):
        wait_for(rz.at[k], rcv.at[6 * NC + 4 * HC + k])
        b1[k, :, :, own_half] = bq[k, z] + rz[k, 1]
        b1[k, :, :, far_half] = rz[k, 0] + rz[k, 2]
        start(r_second, k, par)
        arrive(t_first, k)
        start(t_second, k, par)

    def ret_2(k, par):
        arrive(r_second, k)
        start(r_third, k, par)
        arrive(t_second, k)
        for s in range(SIDE):
            ag[k, s] = lax.dot_general(
                sel1[s], t2[k, s].reshape(256, fc), TN, preferred_element_type=F32
            ).astype(BF)
        t_third(k)

    def ret_3(k, par):
        arrive(r_third, k)
        cols = pl.ds(pl.multiple_of(k * fc, fc), fc)
        out_ref[:, cols] = lax.dot_general(
            sel2[...], rx[k].reshape(512, fc), TN, preferred_element_type=F32
        ).astype(BF)
        wait_for(pr.at[k], rcv.at[6 * NC + 5 * HC + k])
        total = ag[k, z].astype(F32)
        for j in range(3):
            total = total + pr[k, j].astype(F32)
        cols = pl.ds(pl.multiple_of((HC + k) * fc, fc), fc)
        out_ref[:, cols] = total.astype(BF)

    @pl.loop(0, HC)
    def _(i):
        for par in range(2):
            it = 2 * i + par
            for lag, work in (
                (0, ret_0),
                (2, ret_1),
                (2, give_grads),
                (3, ret_2),
                (4, keep_grads),
                (4, ret_3),
            ):

                @pl.when((it >= lag) & (it < HC + lag))
                def _():
                    work(it - lag, (par + lag) % 2)

    for hop, ref in (
        (r_second, ry.at[:, 0:3]),
        (r_third, rx.at[:, 0:3]),
        (t_first, t1.at[:, 0:3]),
        (t_second, t2.at[:, 0:3]),
    ):
        wait_for(ref, leaving(hop, 0))
    wait_for(rz, snd.at[len(hops)])
    wait_for(pr, snd.at[len(hops) + 1])
    for j in (HC - 2, HC - 1):
        gu_send(j).wait_send()
        dn_send(j).wait_send()


PIECES = 4


def hand_on(*refs):
    sem = refs[8]
    copies = []
    for i in range(4):
        src, dst = refs[i], refs[4 + i]
        if i > 0:
            src, dst = src.at[0], dst.at[0]
        part = src.shape[0] // PIECES
        for n in range(PIECES):
            rows = pl.ds(n * part, part)
            copies.append(pltpu.make_async_copy(src.at[rows], dst.at[rows], sem.at[i, n]))
    for copy in copies:
        copy.start()
    for copy in copies:
        copy.wait()


def local(tokens, cotangent, experts, mixing, gate_matrix, up_matrix, down_matrix):
    width = tokens.shape[1]
    ff = gate_matrix.shape[2]
    fc = width // NC
    anywhere = pl.BlockSpec(memory_space=pl.ANY)
    in_vmem = pl.BlockSpec(memory_space=pltpu.VMEM)
    pair_rows = (SIDE, SIDE, 2, ROWS, fc)
    all_rows = (SIDE, SIDE, SIDE, ROWS, fc)
    shapes = (
        jax.ShapeDtypeStruct((TOK, width), BF),
        jax.ShapeDtypeStruct((1, width // 2, ff), F32),
        jax.ShapeDtypeStruct((1, width // 2, ff), F32),
        jax.ShapeDtypeStruct((1, ff // 2, width), F32),
    )
    results = pl.pallas_call(
        kernel,
        out_shape=tuple(pltpu.VMEM(s.shape, s.dtype) for s in shapes),
        in_specs=[in_vmem] * 2 + [anywhere] * 5,
        out_specs=(in_vmem,) * 4,
        scratch_shapes=[
            pltpu.VMEM((NC, TOK, fc), BF),
            pltpu.VMEM((SIDE, 8, TOK), F32),
            pltpu.VMEM((512, TOK), BF),
            pltpu.VMEM((SIDE, 256, TOK), BF),
            pltpu.VMEM((SIDE, 256, 1), F32),
            pltpu.VMEM((NC,) + pair_rows, BF),
            pltpu.VMEM((NC,) + pair_rows, BF),
            pltpu.VMEM((NC,) + pair_rows, BF),
            pltpu.VMEM((NC,) + all_rows, BF),
            pltpu.VMEM((NC, SIDE, TOK, fc), BF),
            pltpu.VMEM((SLOTS,) + all_rows, BF),
            pltpu.VMEM((NC,) + all_rows, BF),
            pltpu.VMEM((NC,) + all_rows, BF),
            pltpu.VMEM((width, ff), BF),
            pltpu.VMEM((width, ff), BF),
            pltpu.VMEM((ff, width), BF),
            pltpu.VMEM((1024, ff), BF),
            pltpu.VMEM((1024, ff), BF),
            pltpu.VMEM((1024, ff), BF),
            pltpu.VMEM((HC, 3, SIDE, SIDE, ROWS, fc), BF),
            pltpu.VMEM((HC,) + pair_rows, BF),
            pltpu.VMEM((HC,) + pair_rows, BF),
            pltpu.VMEM((HC,) + all_rows, BF),
            pltpu.VMEM((HC,) + all_rows, BF),
            pltpu.VMEM((HC, 3, TOK, fc), BF),
            pltpu.VMEM((2, fc, 2 * ff), BF),
            pltpu.VMEM((2, ff // 2, 2 * fc), BF),
            pltpu.VMEM((HC, fc, 2 * ff), BF),
            pltpu.VMEM((HC, ff // 2, 2 * fc), BF),
            pltpu.SemaphoreType.DMA((2,)),
            pltpu.SemaphoreType.DMA((3,)),
            pltpu.SemaphoreType.DMA((2,)),
            pltpu.SemaphoreType.DMA((12 + SLOTS,)),
            pltpu.SemaphoreType.DMA((6 * NC + 6 * HC,)),
            pltpu.SemaphoreType.DMA((2, 2)),
            pltpu.SemaphoreType.DMA((2, HC)),
        ],
        compiler_params=pltpu.CompilerParams(
            collective_id=0, has_side_effects=True, vmem_limit_bytes=56500000
        ),
    )(experts.T, mixing.T, tokens, cotangent, gate_matrix, up_matrix, down_matrix)
    return pl.pallas_call(
        hand_on,
        out_shape=shapes,
        in_specs=[in_vmem] * 4,
        out_specs=(anywhere,) * 4,
        scratch_shapes=[pltpu.SemaphoreType.DMA((4, PIECES))],
        compiler_params=pltpu.CompilerParams(vmem_limit_bytes=1 << 20),
    )(*(pltpu.with_memory_space_constraint(value, pltpu.VMEM) for value in results))


def solution(mesh):
    return jax.shard_map(
        local,
        mesh=mesh,
        in_specs=(
            P(("dp", "expert"), None),
            P(("dp", "expert"), None),
            P(("dp", "expert"), None),
            P(("dp", "expert"), None),
            P("expert", None, None),
            P("expert", None, None),
            P("expert", None, None),
        ),
        out_specs=(
            P(("dp", "expert"), None),
            P("expert", "dp", None),
            P("expert", "dp", None),
            P("expert", "dp", None),
        ),
        check_vma=False,
    )
```

```python
import jax
import jax.numpy as jnp
from jax import lax
from jax.experimental import pallas as pl
from jax.experimental.pallas import tpu as pltpu
from jax.sharding import PartitionSpec as P

MESH = pl.DeviceIdType.MESH
BF = jnp.bfloat16
F32 = jnp.float32
SIDE = 4
ROWS = 16
NC = 8
HC = NC // 2
SLOTS = 3
LAG1 = 1
AHEAD = 3
LAG2 = 3
TOK = 128
NT = (((1,), (1,)), ((), ()))
TN = (((0,), (0,)), ((), ()))


def ranks(meta):
    pair_label = lax.broadcasted_iota(jnp.int32, (32, TOK), 0).astype(F32)
    onehots, names = [], []
    for k in range(4):
        name = meta[k : k + 1, :]
        names.append(name)
        pair = jnp.where(name >= 32.0, name - 32.0, name)
        onehots.append((pair_label == pair).astype(F32))
    count = onehots[0] + onehots[1] + onehots[2] + onehots[3]
    before = (
        lax.broadcasted_iota(jnp.int32, (TOK, TOK), 0)
        < lax.broadcasted_iota(jnp.int32, (TOK, TOK), 1)
    ).astype(BF)
    seen = jnp.dot(count.astype(BF), before, preferred_element_type=F32)
    out = []
    for k in range(4):
        out.append(jnp.sum(onehots[k] * seen, axis=0, keepdims=True))
        seen = seen + onehots[k]
    return names, out


def kernel(
    ids_hbm,
    mix_hbm,
    tok_hbm,
    cot_hbm,
    wg_hbm,
    wu_hbm,
    wd_hbm,
    out_ref,
    gg_ref,
    ug_ref,
    dg_ref,
    ids_ref,
    mix_ref,
    tokv,
    meta_z,
    sel2,
    sel1,
    mix1,
    x2,
    b1,
    b2,
    xf,
    ag,
    dq,
    bq,
    cf,
    wg,
    wu,
    wd,
    gcot,
    ucot,
    hidden,
    rz,
    ry,
    rx,
    t1,
    t2,
    pr,
    pgu,
    pdn,
    qgu,
    qdn,
    in_sem,
    w_sem,
    m_sem,
    snd,
    rcv,
    p_s,
    p_r,
):
    fc = tokv.shape[2]
    ff = gcot.shape[1]
    half_ff = ff // 2
    d = lax.axis_index("dp")
    e = lax.axis_index("expert")
    z = lax.div(e, 16)
    y = lax.rem(lax.div(e, 4), 4)
    x = lax.rem(e, 4)
    other = 1 - d

    def at_z(v):
        return (d, v * 16 + y * 4 + x)

    def at_y(v):
        return (d, z * 16 + v * 4 + x)

    def at_x(v):
        return (d, z * 16 + y * 4 + v)

    def step(v, j):
        return lax.rem(v + j, SIDE)

    def slot(c):
        return lax.rem(c, SLOTS)

    def remote(src, dst, ssem, rsem, dev):
        return pltpu.make_async_remote_copy(
            src_ref=src, dst_ref=dst, send_sem=ssem, recv_sem=rsem, device_id=dev, device_id_type=MESH
        )

    def x_first(c, par):
        if par == 0:
            return x, at_x, lambda v: x2.at[c, v], b1.at[c, x]
        return y, at_y, lambda v: x2.at[c, :, v], b1.at[c, y]

    def x_second(c, par):
        if par == 0:
            return y, at_y, lambda v: b1.at[c, :, v], b2.at[c, y]
        return x, at_x, lambda v: b1.at[c, :, v], b2.at[c, :, x]

    def x_third(c, par):
        return z, at_z, lambda v: b2.at[c, :, :, lax.rem(v, 2)], xf.at[c, z]

    def c_first(c, par):
        return z, at_z, lambda v: ag.at[c, z], ag.at[c, z]

    def c_second(c, par):
        if par == 0:
            return y, at_y, lambda v: dq.at[slot(c), v], bq.at[c, :, y]
        return x, at_x, lambda v: dq.at[slot(c), v], bq.at[c, :, x]

    def c_third(c, par):
        if par == 0:
            return x, at_x, lambda v: bq.at[c, :, :, v], cf.at[c, :, :, x]
        return y, at_y, lambda v: bq.at[c, :, :, v], cf.at[c, :, y]

    def r_second(k, par):
        if par == 0:
            return y, at_y, lambda v: b1.at[k, v], ry.at[k, y]
        return x, at_x, lambda v: b1.at[k, :, v], ry.at[k, x]

    def r_third(k, par):
        if par == 0:
            return x, at_x, lambda v: ry.at[k, :, v], rx.at[k, x]
        return y, at_y, lambda v: ry.at[k, :, v], rx.at[k, :, y]

    def t_first(k, par):
        if par == 0:
            return x, at_x, lambda v: bq.at[HC + k, :, :, v], t1.at[k, :, x]
        return y, at_y, lambda v: bq.at[HC + k, :, v], t1.at[k, :, y]

    def t_second(k, par):
        if par == 0:
            return y, at_y, lambda v: t1.at[k, :, :, v], t2.at[k, :, y]
        return x, at_x, lambda v: t1.at[k, :, :, v], t2.at[k, :, :, x]

    hops = [x_first, x_second, x_third, c_first, c_second, c_third, r_second, r_third, t_first, t_second]

    def landing(hop, c):
        i = hops.index(hop)
        return rcv.at[i * NC + c if i < 6 else 6 * NC + (i - 6) * HC + c]

    def leaving(hop, c):
        return snd.at[len(hops) + 2 + slot(c) if hop is c_second else hops.index(hop)]

    def wait_for(ref, sem):
        pltpu.make_async_copy(ref, ref, sem).wait()

    def start(hop, c, par):
        here, at, src, dst = hop(c, par)
        for j in (1, 3, 2):
            v = step(here, j)
            remote(src(v), dst, leaving(hop, c), landing(hop, c), at(v)).start()
        if hop is not c_first:
            pltpu.make_async_copy(src(here), dst, landing(hop, c)).start()

    def arrive(hop, c):
        ref = (b1, b2, xf, ag, bq, cf, ry, rx, t1, t2)[hops.index(hop)].at[c]
        wait_for(ref.at[0:3] if hop is c_first else ref, landing(hop, c))

    def r_first_to(k, j):
        v = step(z, j)
        sem = rcv.at[6 * NC + 4 * HC + k]
        remote(bq.at[k, v], rz.at[k, j - 1], snd.at[len(hops)], sem, at_z(v)).start()

    def r_first(k):
        for j in (1, 3, 2):
            r_first_to(k, j)

    def t_third(k):
        for j in (1, 3, 2):
            v = step(z, j)
            sem = rcv.at[6 * NC + 5 * HC + k]
            remote(ag.at[k, v], pr.at[k, j - 1], snd.at[len(hops) + 1], sem, at_z(v)).start()

    def tok_in(c):
        cols = pl.ds(pl.multiple_of(c * fc, fc), fc)
        return pltpu.make_async_copy(tok_hbm.at[:, cols], tokv.at[c], in_sem.at[0])

    def cot_in(c):
        cols = pl.ds(pl.multiple_of(c * fc, fc), fc)
        return pltpu.make_async_copy(cot_hbm.at[:, cols], ag.at[c, z], in_sem.at[1])

    weights_in = [
        pltpu.make_async_copy(wg_hbm.at[0], wg, w_sem.at[0]),
        pltpu.make_async_copy(wu_hbm.at[0], wu, w_sem.at[1]),
        pltpu.make_async_copy(wd_hbm.at[0], wd, w_sem.at[2]),
    ]

    barrier = pltpu.get_barrier_semaphore()
    for j in (2, 1, 3):
        for dev in (at_x(step(x, j)), at_y(step(y, j)), at_z(step(z, j))):
            pl.semaphore_signal(barrier, inc=1, device_id=dev, device_id_type=MESH)
    pl.semaphore_signal(barrier, inc=1, device_id=(other, e), device_id_type=MESH)

    ids_in = pltpu.make_async_copy(ids_hbm, ids_ref, w_sem.at[0])
    mix_in = pltpu.make_async_copy(mix_hbm, mix_ref, w_sem.at[1])
    ids_in.start()
    mix_in.start()

    @pl.loop(0, NC)
    def _(c):
        cot_in(c).start()
        tok_in(c).start()

    ids_in.wait()
    mix_in.wait()
    meta_z[z, 0:4, :] = ids_ref[...].astype(F32)
    meta_z[z, 4:8, :] = mix_ref[...]
    names, rank = ranks(ids_ref[...].astype(F32))
    slots = []
    for k in range(4):
        pair = jnp.where(names[k] >= 32.0, names[k] - 32.0, names[k])
        high = (pair >= 16.0).astype(F32)
        rest = pair - 16.0 * high
        row = jnp.floor(rest * 0.25)
        slots.append(((rest - 4.0 * row) * 8.0 + row * 2.0 + high) * ROWS + rank[k])
    slot_label = lax.broadcasted_iota(jnp.int32, (512, TOK), 0).astype(F32)
    picked = (slot_label == slots[0]).astype(F32)
    for k in range(1, 4):
        picked = picked + (slot_label == slots[k]).astype(F32)
    sel2[...] = picked.astype(BF)
    wait_for(tokv, in_sem.at[1])
    wait_for(tokv, in_sem.at[0])
    for copy in weights_in:
        copy.start()

    pl.semaphore_wait(barrier, 10)
    for j in (1, 3, 2):
        v = step(z, j)
        remote(meta_z.at[z], meta_z.at[z], m_sem.at[0], m_sem.at[1], at_z(v)).start()

    def first_hops(c, par):
        start(c_first, c, par)
        rows = jnp.dot(sel2[...], tokv[c], preferred_element_type=F32).astype(BF)
        x2[c] = rows.reshape(SIDE, SIDE, 2, ROWS, fc)
        start(x_first, c, par)

    for c in range(AHEAD):
        first_hops(c, c % 2)
    wait_for(meta_z.at[0:3], m_sem.at[1])
    plane = z.astype(F32) * 16.0
    label1 = lax.broadcasted_iota(jnp.int32, (256, TOK), 0).astype(F32)
    for s in range(SIDE):
        names_s, rank_s = ranks(meta_z[s])
        picked = jnp.zeros((256, TOK), F32)
        mixed = jnp.zeros((256, TOK), F32)
        for k in range(4):
            hit = label1 == (names_s[k] - plane) * ROWS + rank_s[k]
            picked = picked + hit.astype(F32)
            mixed = mixed + jnp.where(hit, meta_z[s, 4 + k : 5 + k, :], 0.0)
        sel1[s] = picked.astype(BF)
        mix1[s] = jnp.sum(mixed, axis=1, keepdims=True)

    for ref in (gg_ref, ug_ref, dg_ref):
        ref[...] = jnp.zeros_like(ref)
    for copy in weights_in:
        copy.wait()

    def second_hops(c, par):
        arrive(x_first, c)
        start(x_second, c, par)
        arrive(c_first, c)

        @pl.when(c >= SLOTS)
        def _():
            wait_for(dq.at[slot(c), 0:3], leaving(c_second, c))

        for s in range(SIDE):
            rows = jnp.dot(sel1[s], ag[c, s], preferred_element_type=F32) * mix1[s]
            rows = rows.astype(BF).reshape(SIDE, SIDE, ROWS, fc)
            if par == 0:
                dq[slot(c), :, s] = rows
            else:
                for v in range(SIDE):
                    dq[slot(c), :, s, v] = rows[v]
        start(c_second, c, par)

        @pl.when(c + AHEAD < NC)
        def _():
            first_hops(c + AHEAD, (par + AHEAD) % 2)

    def third_hops(c, par):
        arrive(x_second, c)
        start(x_third, c, par)
        arrive(c_second, c)
        start(c_third, c, par)

    def multiply(c, par):
        feats = pl.ds(pl.multiple_of(c * fc, fc), fc)
        arrive(x_third, c)
        block = xf[c].reshape(1024, fc)
        for n in range(0, ff, 256):
            units = slice(n, n + 256)
            gg_ref[0, :, units] += jnp.dot(block, wg[feats, units], preferred_element_type=F32)
            ug_ref[0, :, units] += jnp.dot(block, wu[feats, units], preferred_element_type=F32)
        arrive(c_third, c)
        block = cf[c].reshape(1024, fc)
        for u in range(ff // 256):
            value = lax.dot_general(
                block, wd[u * 256 : (u + 1) * 256, feats], NT, preferred_element_type=F32
            )
            for r in range(8):
                dg_ref[0, u * 128 : (u + 1) * 128, r * 256 : (r + 1) * 256] += value[
                    r * 128 : (r + 1) * 128
                ]

    @pl.loop(0, HC + 2)
    def _(i):
        for par in range(2):
            it = 2 * i + par
            for lag, work in ((0, second_hops), (LAG1, third_hops), (LAG2, multiply)):

                @pl.when((it >= lag) & (it < NC + lag))
                def _():
                    work(it - lag, (par + lag) % 2)

    @pl.loop(0, 16)
    def _(i):
        rows = pl.ds(pl.multiple_of(i * 64, 64), 64)
        place = pl.multiple_of(lax.div(i, 2) * 256, 256)
        part = pl.multiple_of(lax.rem(i, 2) * 64, 64)
        for u in range(ff // 256):
            units = slice(u * 256, (u + 1) * 256)
            pre_gate = gg_ref[0, rows, units]
            pre_up = ug_ref[0, rows, units]
            hidden_cot = dg_ref[0, pl.ds(u * 128 + part, 64), pl.ds(place, 256)]
            sigmoid_gate = jax.nn.sigmoid(pre_gate)
            activated = pre_gate * sigmoid_gate
            hidden[rows, units] = (activated * pre_up).astype(BF)
            gcot[rows, units] = (
                hidden_cot * pre_up * sigmoid_gate * (1.0 + pre_gate * (1.0 - sigmoid_gate))
            ).astype(BF)
            ucot[rows, units] = (hidden_cot * activated).astype(BF)

    for hop, ref in (
        (x_first, x2.at[:, 0:3]),
        (x_second, b2.at[:, 0:3]),
        (x_third, xf.at[:, 0:3]),
        (c_first, ag.at[:, 0:3]),
        (c_third, cf.at[:, 0:3]),
    ):
        wait_for(ref, leaving(hop, 0))
    for c in range(NC - SLOTS, NC):
        wait_for(dq.at[slot(c), 0:3], leaving(c_second, c))
    wait_for(meta_z.at[0:3], m_sem.at[0])

    own_half = lax.rem(z, 2)
    far_half = 1 - own_half

    def gu_send(j):
        return remote(pgu.at[lax.rem(j, 2)], qgu.at[j], p_s.at[0, lax.rem(j, 2)], p_r.at[0, j], (other, e))

    def dn_send(j):
        return remote(pdn.at[lax.rem(j, 2)], qdn.at[j], p_s.at[1, lax.rem(j, 2)], p_r.at[1, j], (other, e))

    def grads(j, side, store_gu, store_dn):
        c = side * HC + j
        left = xf[c].reshape(1024, fc)
        store_gu(0, lax.dot_general(left, gcot[...], TN, preferred_element_type=F32))
        store_gu(1, lax.dot_general(left, ucot[...], TN, preferred_element_type=F32))
        units = pl.ds(pl.multiple_of(side * half_ff, 128), half_ff)
        for b in range(2):
            right = cf[2 * j + b].reshape(1024, fc)
            store_dn(
                b, lax.dot_general(hidden[:, units], right, TN, preferred_element_type=F32)
            )

    def back(c):
        feats = pl.ds(pl.multiple_of(c * fc, fc), fc)
        value = lax.dot_general(
            gcot[...], wg[feats, :], NT, preferred_element_type=F32
        ) + lax.dot_general(ucot[...], wu[feats, :], NT, preferred_element_type=F32)
        bq[c] = value.astype(BF).reshape(SIDE, SIDE, SIDE, ROWS, fc)

    def ret_0(k, par):
        if par == 0:

            @pl.when(k == 0)
            def _():
                feats = pl.ds(0, fc)
                for j in (2, 1, 3, 0):
                    v = step(z, j)
                    rows = pl.ds(pl.multiple_of(v * 256, 256), 256)
                    value = lax.dot_general(
                        gcot[rows, :], wg[feats, :], NT, preferred_element_type=F32
                    ) + lax.dot_general(
                        ucot[rows, :], wu[feats, :], NT, preferred_element_type=F32
                    )
                    bq[0, v] = value.astype(BF).reshape(SIDE, SIDE, ROWS, fc)
                    if j > 0:
                        r_first_to(0, j)

            @pl.when(k > 0)
            def _():
                back(k)
                r_first(k)
        else:
            back(k)
            r_first(k)
        back(HC + k)
        start(t_first, k, par)

    def give_grads(j, par):
        @pl.when(j >= 2)
        def _():
            gu_send(j - 2).wait_send()
            dn_send(j - 2).wait_send()

        def store_gu(which, value):
            pgu[lax.rem(j, 2), :, which * ff : (which + 1) * ff] = value.astype(BF)

        def store_dn(b, value):
            pdn[lax.rem(j, 2), :, b * fc : (b + 1) * fc] = value.astype(BF)

        grads(j, other, store_gu, store_dn)
        gu_send(j).start()
        dn_send(j).start()

    def keep_grads(j, par):
        gu_send(j).wait_recv()
        dn_send(j).wait_recv()

        rows = pl.ds(pl.multiple_of(j * fc, fc), fc)

        def store_gu(which, value):
            ref = (gg_ref, ug_ref)[which]
            ref[0, rows, :] = value + qgu[j, :, which * ff : (which + 1) * ff].astype(F32)

        def store_dn(b, value):
            cols = pl.ds(pl.multiple_of((2 * j + b) * fc, fc), fc)
            dg_ref[0, :, cols] = value + qdn[j, :, b * fc : (b + 1) * fc].astype(F32)

        grads(j, d, store_gu, store_dn)

    def ret_1(k, par):
        wait_for(rz.at[k], rcv.at[6 * NC + 4 * HC + k])
        b1[k, :, :, own_half] = bq[k, z] + rz[k, 1]
        b1[k, :, :, far_half] = rz[k, 0] + rz[k, 2]
        start(r_second, k, par)
        arrive(t_first, k)
        start(t_second, k, par)

    def ret_2(k, par):
        arrive(r_second, k)
        start(r_third, k, par)
        arrive(t_second, k)
        for s in range(SIDE):
            ag[k, s] = lax.dot_general(
                sel1[s], t2[k, s].reshape(256, fc), TN, preferred_element_type=F32
            ).astype(BF)
        t_third(k)

    def ret_3(k, par):
        arrive(r_third, k)
        cols = pl.ds(pl.multiple_of(k * fc, fc), fc)
        out_ref[:, cols] = lax.dot_general(
            sel2[...], rx[k].reshape(512, fc), TN, preferred_element_type=F32
        ).astype(BF)
        wait_for(pr.at[k], rcv.at[6 * NC + 5 * HC + k])
        total = ag[k, z].astype(F32)
        for j in range(3):
            total = total + pr[k, j].astype(F32)
        cols = pl.ds(pl.multiple_of((HC + k) * fc, fc), fc)
        out_ref[:, cols] = total.astype(BF)

    @pl.loop(0, HC)
    def _(i):
        for par in range(2):
            it = 2 * i + par
            for lag, work in (
                (0, ret_0),
                (2, ret_1),
                (2, give_grads),
                (3, ret_2),
                (4, keep_grads),
                (4, ret_3),
            ):

                @pl.when((it >= lag) & (it < HC + lag))
                def _():
                    work(it - lag, (par + lag) % 2)

    for hop, ref in (
        (r_second, ry.at[:, 0:3]),
        (r_third, rx.at[:, 0:3]),
        (t_first, t1.at[:, 0:3]),
        (t_second, t2.at[:, 0:3]),
    ):
        wait_for(ref, leaving(hop, 0))
    wait_for(rz, snd.at[len(hops)])
    wait_for(pr, snd.at[len(hops) + 1])
    for j in (HC - 2, HC - 1):
        gu_send(j).wait_send()
        dn_send(j).wait_send()


PIECES = 4


def hand_on(*refs):
    sem = refs[8]
    copies = []
    for i in range(4):
        src, dst = refs[i], refs[4 + i]
        if i > 0:
            src, dst = src.at[0], dst.at[0]
        part = src.shape[0] // PIECES
        for n in range(PIECES):
            rows = pl.ds(n * part, part)
            copies.append(pltpu.make_async_copy(src.at[rows], dst.at[rows], sem.at[i, n]))
    for copy in copies:
        copy.start()
    for copy in copies:
        copy.wait()


def local(tokens, cotangent, experts, mixing, gate_matrix, up_matrix, down_matrix):
    width = tokens.shape[1]
    ff = gate_matrix.shape[2]
    fc = width // NC
    anywhere = pl.BlockSpec(memory_space=pl.ANY)
    in_vmem = pl.BlockSpec(memory_space=pltpu.VMEM)
    pair_rows = (SIDE, SIDE, 2, ROWS, fc)
    all_rows = (SIDE, SIDE, SIDE, ROWS, fc)
    shapes = (
        jax.ShapeDtypeStruct((TOK, width), BF),
        jax.ShapeDtypeStruct((1, width // 2, ff), F32),
        jax.ShapeDtypeStruct((1, width // 2, ff), F32),
        jax.ShapeDtypeStruct((1, ff // 2, width), F32),
    )
    results = pl.pallas_call(
        kernel,
        out_shape=tuple(pltpu.VMEM(s.shape, s.dtype) for s in shapes),
        in_specs=[anywhere] * 7,
        out_specs=(in_vmem,) * 4,
        scratch_shapes=[
            pltpu.VMEM((4, TOK), jnp.int32),
            pltpu.VMEM((4, TOK), F32),
            pltpu.VMEM((NC, TOK, fc), BF),
            pltpu.VMEM((SIDE, 8, TOK), F32),
            pltpu.VMEM((512, TOK), BF),
            pltpu.VMEM((SIDE, 256, TOK), BF),
            pltpu.VMEM((SIDE, 256, 1), F32),
            pltpu.VMEM((NC,) + pair_rows, BF),
            pltpu.VMEM((NC,) + pair_rows, BF),
            pltpu.VMEM((NC,) + pair_rows, BF),
            pltpu.VMEM((NC,) + all_rows, BF),
            pltpu.VMEM((NC, SIDE, TOK, fc), BF),
            pltpu.VMEM((SLOTS,) + all_rows, BF),
            pltpu.VMEM((NC,) + all_rows, BF),
            pltpu.VMEM((NC,) + all_rows, BF),
            pltpu.VMEM((width, ff), BF),
            pltpu.VMEM((width, ff), BF),
            pltpu.VMEM((ff, width), BF),
            pltpu.VMEM((1024, ff), BF),
            pltpu.VMEM((1024, ff), BF),
            pltpu.VMEM((1024, ff), BF),
            pltpu.VMEM((HC, 3, SIDE, SIDE, ROWS, fc), BF),
            pltpu.VMEM((HC,) + pair_rows, BF),
            pltpu.VMEM((HC,) + pair_rows, BF),
            pltpu.VMEM((HC,) + all_rows, BF),
            pltpu.VMEM((HC,) + all_rows, BF),
            pltpu.VMEM((HC, 3, TOK, fc), BF),
            pltpu.VMEM((2, fc, 2 * ff), BF),
            pltpu.VMEM((2, ff // 2, 2 * fc), BF),
            pltpu.VMEM((HC, fc, 2 * ff), BF),
            pltpu.VMEM((HC, ff // 2, 2 * fc), BF),
            pltpu.SemaphoreType.DMA((2,)),
            pltpu.SemaphoreType.DMA((3,)),
            pltpu.SemaphoreType.DMA((2,)),
            pltpu.SemaphoreType.DMA((12 + SLOTS,)),
            pltpu.SemaphoreType.DMA((6 * NC + 6 * HC,)),
            pltpu.SemaphoreType.DMA((2, 2)),
            pltpu.SemaphoreType.DMA((2, HC)),
        ],
        compiler_params=pltpu.CompilerParams(
            collective_id=0, has_side_effects=True, vmem_limit_bytes=56500000
        ),
    )(experts.T, mixing.T, tokens, cotangent, gate_matrix, up_matrix, down_matrix)
    return pl.pallas_call(
        hand_on,
        out_shape=shapes,
        in_specs=[in_vmem] * 4,
        out_specs=(anywhere,) * 4,
        scratch_shapes=[pltpu.SemaphoreType.DMA((4, PIECES))],
        compiler_params=pltpu.CompilerParams(vmem_limit_bytes=1 << 20),
    )(*(pltpu.with_memory_space_constraint(value, pltpu.VMEM) for value in results))


def solution(mesh):
    return jax.shard_map(
        local,
        mesh=mesh,
        in_specs=(
            P(("dp", "expert"), None),
            P(("dp", "expert"), None),
            P(("dp", "expert"), None),
            P(("dp", "expert"), None),
            P("expert", None, None),
            P("expert", None, None),
            P("expert", None, None),
        ),
        out_specs=(
            P(("dp", "expert"), None),
            P("expert", "dp", None),
            P("expert", "dp", None),
            P("expert", "dp", None),
        ),
        check_vma=False,
    )
```

```python
import jax
import jax.numpy as jnp
from jax import lax
from jax.experimental import pallas as pl
from jax.experimental.pallas import tpu as pltpu
from jax.sharding import PartitionSpec as P

MESH = pl.DeviceIdType.MESH
BF = jnp.bfloat16
F32 = jnp.float32
SIDE = 4
ROWS = 16
NC = 8
HC = NC // 2
SLOTS = 3
LAG1 = 1
AHEAD = 3
LAG2 = 3
TOK = 128
NT = (((1,), (1,)), ((), ()))
TN = (((0,), (0,)), ((), ()))


def ranks(meta):
    pair_label = lax.broadcasted_iota(jnp.int32, (32, TOK), 0).astype(F32)
    onehots, names = [], []
    for k in range(4):
        name = meta[k : k + 1, :]
        names.append(name)
        pair = jnp.where(name >= 32.0, name - 32.0, name)
        onehots.append((pair_label == pair).astype(F32))
    count = onehots[0] + onehots[1] + onehots[2] + onehots[3]
    before = (
        lax.broadcasted_iota(jnp.int32, (TOK, TOK), 0)
        < lax.broadcasted_iota(jnp.int32, (TOK, TOK), 1)
    ).astype(BF)
    seen = jnp.dot(count.astype(BF), before, preferred_element_type=F32)
    out = []
    for k in range(4):
        out.append(jnp.sum(onehots[k] * seen, axis=0, keepdims=True))
        seen = seen + onehots[k]
    return names, out


def kernel(
    ids_hbm,
    mix_hbm,
    tok_hbm,
    cot_hbm,
    wg_hbm,
    wu_hbm,
    wd_hbm,
    out_ref,
    gg_ref,
    ug_ref,
    dg_ref,
    ids_ref,
    mix_ref,
    tokv,
    meta_z,
    sel2,
    sel1,
    mix1,
    x2,
    b1,
    b2,
    xf,
    ag,
    dq,
    bq,
    cf,
    wg,
    wu,
    wd,
    gcot,
    ucot,
    hidden,
    rz,
    ry,
    rx,
    t1,
    t2,
    pr,
    pgu,
    pdn,
    qgu,
    qdn,
    in_sem,
    w_sem,
    m_sem,
    snd,
    rcv,
    p_s,
    p_r,
):
    fc = tokv.shape[2]
    ff = gcot.shape[1]
    half_ff = ff // 2
    d = lax.axis_index("dp")
    e = lax.axis_index("expert")
    z = lax.div(e, 16)
    y = lax.rem(lax.div(e, 4), 4)
    x = lax.rem(e, 4)
    other = 1 - d

    def at_z(v):
        return (d, v * 16 + y * 4 + x)

    def at_y(v):
        return (d, z * 16 + v * 4 + x)

    def at_x(v):
        return (d, z * 16 + y * 4 + v)

    def step(v, j):
        return lax.rem(v + j, SIDE)

    def slot(c):
        return lax.rem(c, SLOTS)

    def remote(src, dst, ssem, rsem, dev):
        return pltpu.make_async_remote_copy(
            src_ref=src, dst_ref=dst, send_sem=ssem, recv_sem=rsem, device_id=dev, device_id_type=MESH
        )

    def x_first(c, par):
        if par == 0:
            return x, at_x, lambda v: x2.at[c, v], b1.at[c, x]
        return y, at_y, lambda v: x2.at[c, :, v], b1.at[c, y]

    def x_second(c, par):
        if par == 0:
            return y, at_y, lambda v: b1.at[c, :, v], b2.at[c, y]
        return x, at_x, lambda v: b1.at[c, :, v], b2.at[c, :, x]

    def x_third(c, par):
        return z, at_z, lambda v: b2.at[c, :, :, lax.rem(v, 2)], xf.at[c, z]

    def c_first(c, par):
        return z, at_z, lambda v: ag.at[c, z], ag.at[c, z]

    def c_second(c, par):
        if par == 0:
            return y, at_y, lambda v: dq.at[slot(c), v], bq.at[c, :, y]
        return x, at_x, lambda v: dq.at[slot(c), v], bq.at[c, :, x]

    def c_third(c, par):
        if par == 0:
            return x, at_x, lambda v: bq.at[c, :, :, v], cf.at[c, :, :, x]
        return y, at_y, lambda v: bq.at[c, :, :, v], cf.at[c, :, y]

    def r_second(k, par):
        if par == 0:
            return y, at_y, lambda v: b1.at[k, v], ry.at[k, y]
        return x, at_x, lambda v: b1.at[k, :, v], ry.at[k, x]

    def r_third(k, par):
        if par == 0:
            return x, at_x, lambda v: ry.at[k, :, v], rx.at[k, x]
        return y, at_y, lambda v: ry.at[k, :, v], rx.at[k, :, y]

    def t_first(k, par):
        if par == 0:
            return x, at_x, lambda v: bq.at[HC + k, :, :, v], t1.at[k, :, x]
        return y, at_y, lambda v: bq.at[HC + k, :, v], t1.at[k, :, y]

    def t_second(k, par):
        if par == 0:
            return y, at_y, lambda v: t1.at[k, :, :, v], t2.at[k, :, y]
        return x, at_x, lambda v: t1.at[k, :, :, v], t2.at[k, :, :, x]

    hops = [x_first, x_second, x_third, c_first, c_second, c_third, r_second, r_third, t_first, t_second]

    def landing(hop, c):
        i = hops.index(hop)
        return rcv.at[i * NC + c if i < 6 else 6 * NC + (i - 6) * HC + c]

    def leaving(hop, c):
        return snd.at[len(hops) + 2 + slot(c) if hop is c_second else hops.index(hop)]

    def wait_for(ref, sem):
        pltpu.make_async_copy(ref, ref, sem).wait()

    def start(hop, c, par):
        here, at, src, dst = hop(c, par)
        for j in (1, 3, 2):
            v = step(here, j)
            remote(src(v), dst, leaving(hop, c), landing(hop, c), at(v)).start()
        if hop is not c_first:
            pltpu.make_async_copy(src(here), dst, landing(hop, c)).start()

    def arrive(hop, c):
        ref = (b1, b2, xf, ag, bq, cf, ry, rx, t1, t2)[hops.index(hop)].at[c]
        wait_for(ref.at[0:3] if hop is c_first else ref, landing(hop, c))

    def r_first_to(k, j):
        v = step(z, j)
        sem = rcv.at[6 * NC + 4 * HC + k]
        remote(bq.at[k, v], rz.at[k, j - 1], snd.at[len(hops)], sem, at_z(v)).start()

    def r_first(k):
        for j in (1, 3, 2):
            r_first_to(k, j)

    def t_third(k):
        for j in (1, 3, 2):
            v = step(z, j)
            sem = rcv.at[6 * NC + 5 * HC + k]
            remote(ag.at[k, v], pr.at[k, j - 1], snd.at[len(hops) + 1], sem, at_z(v)).start()

    def tok_in(c):
        cols = pl.ds(pl.multiple_of(c * fc, fc), fc)
        return pltpu.make_async_copy(tok_hbm.at[:, cols], tokv.at[c], in_sem.at[0])

    def cot_in(c):
        cols = pl.ds(pl.multiple_of(c * fc, fc), fc)
        return pltpu.make_async_copy(cot_hbm.at[:, cols], ag.at[c, z], in_sem.at[1])

    weights_in = [
        pltpu.make_async_copy(wg_hbm.at[0], wg, w_sem.at[0]),
        pltpu.make_async_copy(wu_hbm.at[0], wu, w_sem.at[1]),
        pltpu.make_async_copy(wd_hbm.at[0], wd, w_sem.at[2]),
    ]

    barrier = pltpu.get_barrier_semaphore()
    for j in (2, 1, 3):
        for dev in (at_x(step(x, j)), at_y(step(y, j)), at_z(step(z, j))):
            pl.semaphore_signal(barrier, inc=1, device_id=dev, device_id_type=MESH)
    pl.semaphore_signal(barrier, inc=1, device_id=(other, e), device_id_type=MESH)

    ids_in = pltpu.make_async_copy(ids_hbm, ids_ref, w_sem.at[0])
    mix_in = pltpu.make_async_copy(mix_hbm, mix_ref, w_sem.at[1])
    ids_in.start()
    mix_in.start()

    @pl.loop(0, NC)
    def _(c):
        cot_in(c).start()
        tok_in(c).start()

    ids_in.wait()
    mix_in.wait()
    meta_z[z, 0:4, :] = ids_ref[...].astype(F32)
    meta_z[z, 4:8, :] = mix_ref[...]
    names, rank = ranks(ids_ref[...].astype(F32))
    slots = []
    for k in range(4):
        pair = jnp.where(names[k] >= 32.0, names[k] - 32.0, names[k])
        high = (pair >= 16.0).astype(F32)
        rest = pair - 16.0 * high
        row = jnp.floor(rest * 0.25)
        slots.append(((rest - 4.0 * row) * 8.0 + row * 2.0 + high) * ROWS + rank[k])
    slot_label = lax.broadcasted_iota(jnp.int32, (512, TOK), 0).astype(F32)
    picked = (slot_label == slots[0]).astype(F32)
    for k in range(1, 4):
        picked = picked + (slot_label == slots[k]).astype(F32)
    sel2[...] = picked.astype(BF)
    wait_for(tokv, in_sem.at[1])
    wait_for(tokv, in_sem.at[0])
    for copy in weights_in:
        copy.start()

    pl.semaphore_wait(barrier, 10)
    for j in (1, 3, 2):
        v = step(z, j)
        remote(meta_z.at[z], meta_z.at[z], m_sem.at[0], m_sem.at[1], at_z(v)).start()

    def first_hops(c, par):
        start(c_first, c, par)
        rows = jnp.dot(sel2[...], tokv[c], preferred_element_type=F32).astype(BF)
        x2[c] = rows.reshape(SIDE, SIDE, 2, ROWS, fc)
        start(x_first, c, par)

    for c in range(AHEAD):
        first_hops(c, c % 2)
    wait_for(meta_z.at[0:3], m_sem.at[1])
    plane = z.astype(F32) * 16.0
    label1 = lax.broadcasted_iota(jnp.int32, (256, TOK), 0).astype(F32)
    for s in range(SIDE):
        names_s, rank_s = ranks(meta_z[s])
        picked = jnp.zeros((256, TOK), F32)
        mixed = jnp.zeros((256, TOK), F32)
        for k in range(4):
            hit = label1 == (names_s[k] - plane) * ROWS + rank_s[k]
            picked = picked + hit.astype(F32)
            mixed = mixed + jnp.where(hit, meta_z[s, 4 + k : 5 + k, :], 0.0)
        sel1[s] = picked.astype(BF)
        mix1[s] = jnp.sum(mixed, axis=1, keepdims=True)

    for ref in (gg_ref, ug_ref, dg_ref):
        ref[...] = jnp.zeros_like(ref)
    for copy in weights_in:
        copy.wait()

    def second_hops(c, par):
        arrive(x_first, c)
        start(x_second, c, par)
        arrive(c_first, c)

        @pl.when(c >= SLOTS)
        def _():
            wait_for(dq.at[slot(c), 0:3], leaving(c_second, c))

        for s in range(SIDE):
            rows = jnp.dot(sel1[s], ag[c, s], preferred_element_type=F32) * mix1[s]
            rows = rows.astype(BF).reshape(SIDE, SIDE, ROWS, fc)
            if par == 0:
                dq[slot(c), :, s] = rows
            else:
                for v in range(SIDE):
                    dq[slot(c), :, s, v] = rows[v]
        start(c_second, c, par)

        @pl.when(c + AHEAD < NC)
        def _():
            first_hops(c + AHEAD, (par + AHEAD) % 2)

    def third_hops(c, par):
        arrive(x_second, c)
        start(x_third, c, par)
        arrive(c_second, c)
        start(c_third, c, par)

    def multiply(c, par):
        feats = pl.ds(pl.multiple_of(c * fc, fc), fc)
        arrive(x_third, c)
        block = xf[c].reshape(1024, fc)
        for n in range(0, ff, 256):
            units = slice(n, n + 256)
            gg_ref[0, :, units] += jnp.dot(block, wg[feats, units], preferred_element_type=F32)
            ug_ref[0, :, units] += jnp.dot(block, wu[feats, units], preferred_element_type=F32)
        arrive(c_third, c)
        block = cf[c].reshape(1024, fc)
        for u in range(ff // 256):
            value = lax.dot_general(
                block, wd[u * 256 : (u + 1) * 256, feats], NT, preferred_element_type=F32
            )
            for r in range(8):
                dg_ref[0, u * 128 : (u + 1) * 128, r * 256 : (r + 1) * 256] += value[
                    r * 128 : (r + 1) * 128
                ]

    @pl.loop(0, HC + 2)
    def _(i):
        for par in range(2):
            it = 2 * i + par
            for lag, work in ((0, second_hops), (LAG1, third_hops), (LAG2, multiply)):

                @pl.when((it >= lag) & (it < NC + lag))
                def _():
                    work(it - lag, (par + lag) % 2)

    @pl.loop(0, 16)
    def _(i):
        rows = pl.ds(pl.multiple_of(i * 64, 64), 64)
        place = pl.multiple_of(lax.div(i, 2) * 256, 256)
        part = pl.multiple_of(lax.rem(i, 2) * 64, 64)
        for u in range(ff // 256):
            units = slice(u * 256, (u + 1) * 256)
            pre_gate = gg_ref[0, rows, units]
            pre_up = ug_ref[0, rows, units]
            hidden_cot = dg_ref[0, pl.ds(u * 128 + part, 64), pl.ds(place, 256)]
            sigmoid_gate = jax.nn.sigmoid(pre_gate)
            activated = pre_gate * sigmoid_gate
            hidden[rows, units] = (activated * pre_up).astype(BF)
            gcot[rows, units] = (
                hidden_cot * pre_up * sigmoid_gate * (1.0 + pre_gate * (1.0 - sigmoid_gate))
            ).astype(BF)
            ucot[rows, units] = (hidden_cot * activated).astype(BF)

    for hop, ref in (
        (x_first, x2.at[:, 0:3]),
        (x_second, b2.at[:, 0:3]),
        (x_third, xf.at[:, 0:3]),
        (c_first, ag.at[:, 0:3]),
        (c_third, cf.at[:, 0:3]),
    ):
        wait_for(ref, leaving(hop, 0))
    for c in range(NC - SLOTS, NC):
        wait_for(dq.at[slot(c), 0:3], leaving(c_second, c))
    wait_for(meta_z.at[0:3], m_sem.at[0])

    own_half = lax.rem(z, 2)
    far_half = 1 - own_half

    def gu_send(j):
        return remote(pgu.at[lax.rem(j, 2)], qgu.at[j], p_s.at[0, lax.rem(j, 2)], p_r.at[0, j], (other, e))

    def dn_send(j):
        return remote(pdn.at[lax.rem(j, 2)], qdn.at[j], p_s.at[1, lax.rem(j, 2)], p_r.at[1, j], (other, e))

    def grads(j, side, store_gu, store_dn):
        c = side * HC + j
        left = xf[c].reshape(1024, fc)
        store_gu(0, lax.dot_general(left, gcot[...], TN, preferred_element_type=F32))
        store_gu(1, lax.dot_general(left, ucot[...], TN, preferred_element_type=F32))
        units = pl.ds(pl.multiple_of(side * half_ff, 128), half_ff)
        for b in range(2):
            right = cf[2 * j + b].reshape(1024, fc)
            store_dn(
                b, lax.dot_general(hidden[:, units], right, TN, preferred_element_type=F32)
            )

    def back(c):
        feats = pl.ds(pl.multiple_of(c * fc, fc), fc)
        value = lax.dot_general(
            gcot[...], wg[feats, :], NT, preferred_element_type=F32
        ) + lax.dot_general(ucot[...], wu[feats, :], NT, preferred_element_type=F32)
        bq[c] = value.astype(BF).reshape(SIDE, SIDE, SIDE, ROWS, fc)

    def ret_0(k, par):
        if par == 0:

            @pl.when(k == 0)
            def _():
                feats = pl.ds(0, fc)
                for j in (2, 1, 3, 0):
                    v = step(z, j)
                    rows = pl.ds(pl.multiple_of(v * 256, 256), 256)
                    value = lax.dot_general(
                        gcot[rows, :], wg[feats, :], NT, preferred_element_type=F32
                    ) + lax.dot_general(
                        ucot[rows, :], wu[feats, :], NT, preferred_element_type=F32
                    )
                    bq[0, v] = value.astype(BF).reshape(SIDE, SIDE, ROWS, fc)
                    if j > 0:
                        r_first_to(0, j)

            @pl.when(k > 0)
            def _():
                back(k)
                r_first(k)
        else:
            back(k)
            r_first(k)
        back(HC + k)
        start(t_first, k, par)

    def give_grads(j, par):
        @pl.when(j >= 2)
        def _():
            gu_send(j - 2).wait_send()
            dn_send(j - 2).wait_send()

        def store_gu(which, value):
            pgu[lax.rem(j, 2), :, which * ff : (which + 1) * ff] = value.astype(BF)

        def store_dn(b, value):
            pdn[lax.rem(j, 2), :, b * fc : (b + 1) * fc] = value.astype(BF)

        grads(j, other, store_gu, store_dn)
        gu_send(j).start()
        dn_send(j).start()

    def keep_grads(j, par):
        gu_send(j).wait_recv()
        dn_send(j).wait_recv()

        rows = pl.ds(pl.multiple_of(j * fc, fc), fc)

        def store_gu(which, value):
            ref = (gg_ref, ug_ref)[which]
            ref[0, rows, :] = value + qgu[j, :, which * ff : (which + 1) * ff].astype(F32)

        def store_dn(b, value):
            cols = pl.ds(pl.multiple_of((2 * j + b) * fc, fc), fc)
            dg_ref[0, :, cols] = value + qdn[j, :, b * fc : (b + 1) * fc].astype(F32)

        grads(j, d, store_gu, store_dn)

    def ret_1(k, par):
        wait_for(rz.at[k], rcv.at[6 * NC + 4 * HC + k])
        b1[k, :, :, own_half] = bq[k, z] + rz[k, 1]
        b1[k, :, :, far_half] = rz[k, 0] + rz[k, 2]
        start(r_second, k, par)
        arrive(t_first, k)
        start(t_second, k, par)

    def ret_2(k, par):
        arrive(r_second, k)
        start(r_third, k, par)
        arrive(t_second, k)
        for s in range(SIDE):
            ag[k, s] = lax.dot_general(
                sel1[s], t2[k, s].reshape(256, fc), TN, preferred_element_type=F32
            ).astype(BF)
        t_third(k)

    def ret_3(k, par):
        arrive(r_third, k)
        cols = pl.ds(pl.multiple_of(k * fc, fc), fc)
        out_ref[:, cols] = lax.dot_general(
            sel2[...], rx[k].reshape(512, fc), TN, preferred_element_type=F32
        ).astype(BF)
        wait_for(pr.at[k], rcv.at[6 * NC + 5 * HC + k])
        total = ag[k, z].astype(F32)
        for j in range(3):
            total = total + pr[k, j].astype(F32)
        cols = pl.ds(pl.multiple_of((HC + k) * fc, fc), fc)
        out_ref[:, cols] = total.astype(BF)

    @pl.loop(0, HC)
    def _(i):
        for par in range(2):
            it = 2 * i + par
            for lag, work in (
                (0, ret_0),
                (2, give_grads),
                (2, ret_1),
                (3, ret_2),
                (4, keep_grads),
                (4, ret_3),
            ):

                @pl.when((it >= lag) & (it < HC + lag))
                def _():
                    work(it - lag, (par + lag) % 2)

    for hop, ref in (
        (r_second, ry.at[:, 0:3]),
        (r_third, rx.at[:, 0:3]),
        (t_first, t1.at[:, 0:3]),
        (t_second, t2.at[:, 0:3]),
    ):
        wait_for(ref, leaving(hop, 0))
    wait_for(rz, snd.at[len(hops)])
    wait_for(pr, snd.at[len(hops) + 1])
    for j in (HC - 2, HC - 1):
        gu_send(j).wait_send()
        dn_send(j).wait_send()


PIECES = 4


def hand_on(*refs):
    sem = refs[8]
    copies = []
    for i in range(4):
        src, dst = refs[i], refs[4 + i]
        if i > 0:
            src, dst = src.at[0], dst.at[0]
        part = src.shape[0] // PIECES
        for n in range(PIECES):
            rows = pl.ds(n * part, part)
            copies.append(pltpu.make_async_copy(src.at[rows], dst.at[rows], sem.at[i, n]))
    for copy in copies:
        copy.start()
    for copy in copies:
        copy.wait()


def local(tokens, cotangent, experts, mixing, gate_matrix, up_matrix, down_matrix):
    width = tokens.shape[1]
    ff = gate_matrix.shape[2]
    fc = width // NC
    anywhere = pl.BlockSpec(memory_space=pl.ANY)
    in_vmem = pl.BlockSpec(memory_space=pltpu.VMEM)
    pair_rows = (SIDE, SIDE, 2, ROWS, fc)
    all_rows = (SIDE, SIDE, SIDE, ROWS, fc)
    shapes = (
        jax.ShapeDtypeStruct((TOK, width), BF),
        jax.ShapeDtypeStruct((1, width // 2, ff), F32),
        jax.ShapeDtypeStruct((1, width // 2, ff), F32),
        jax.ShapeDtypeStruct((1, ff // 2, width), F32),
    )
    results = pl.pallas_call(
        kernel,
        out_shape=tuple(pltpu.VMEM(s.shape, s.dtype) for s in shapes),
        in_specs=[anywhere] * 7,
        out_specs=(in_vmem,) * 4,
        scratch_shapes=[
            pltpu.VMEM((4, TOK), jnp.int32),
            pltpu.VMEM((4, TOK), F32),
            pltpu.VMEM((NC, TOK, fc), BF),
            pltpu.VMEM((SIDE, 8, TOK), F32),
            pltpu.VMEM((512, TOK), BF),
            pltpu.VMEM((SIDE, 256, TOK), BF),
            pltpu.VMEM((SIDE, 256, 1), F32),
            pltpu.VMEM((NC,) + pair_rows, BF),
            pltpu.VMEM((NC,) + pair_rows, BF),
            pltpu.VMEM((NC,) + pair_rows, BF),
            pltpu.VMEM((NC,) + all_rows, BF),
            pltpu.VMEM((NC, SIDE, TOK, fc), BF),
            pltpu.VMEM((SLOTS,) + all_rows, BF),
            pltpu.VMEM((NC,) + all_rows, BF),
            pltpu.VMEM((NC,) + all_rows, BF),
            pltpu.VMEM((width, ff), BF),
            pltpu.VMEM((width, ff), BF),
            pltpu.VMEM((ff, width), BF),
            pltpu.VMEM((1024, ff), BF),
            pltpu.VMEM((1024, ff), BF),
            pltpu.VMEM((1024, ff), BF),
            pltpu.VMEM((HC, 3, SIDE, SIDE, ROWS, fc), BF),
            pltpu.VMEM((HC,) + pair_rows, BF),
            pltpu.VMEM((HC,) + pair_rows, BF),
            pltpu.VMEM((HC,) + all_rows, BF),
            pltpu.VMEM((HC,) + all_rows, BF),
            pltpu.VMEM((HC, 3, TOK, fc), BF),
            pltpu.VMEM((2, fc, 2 * ff), BF),
            pltpu.VMEM((2, ff // 2, 2 * fc), BF),
            pltpu.VMEM((HC, fc, 2 * ff), BF),
            pltpu.VMEM((HC, ff // 2, 2 * fc), BF),
            pltpu.SemaphoreType.DMA((2,)),
            pltpu.SemaphoreType.DMA((3,)),
            pltpu.SemaphoreType.DMA((2,)),
            pltpu.SemaphoreType.DMA((12 + SLOTS,)),
            pltpu.SemaphoreType.DMA((6 * NC + 6 * HC,)),
            pltpu.SemaphoreType.DMA((2, 2)),
            pltpu.SemaphoreType.DMA((2, HC)),
        ],
        compiler_params=pltpu.CompilerParams(
            collective_id=0, has_side_effects=True, vmem_limit_bytes=56500000
        ),
    )(experts.T, mixing.T, tokens, cotangent, gate_matrix, up_matrix, down_matrix)
    return pl.pallas_call(
        hand_on,
        out_shape=shapes,
        in_specs=[in_vmem] * 4,
        out_specs=(anywhere,) * 4,
        scratch_shapes=[pltpu.SemaphoreType.DMA((4, PIECES))],
        compiler_params=pltpu.CompilerParams(vmem_limit_bytes=1 << 20),
    )(*(pltpu.with_memory_space_constraint(value, pltpu.VMEM) for value in results))


def solution(mesh):
    return jax.shard_map(
        local,
        mesh=mesh,
        in_specs=(
            P(("dp", "expert"), None),
            P(("dp", "expert"), None),
            P(("dp", "expert"), None),
            P(("dp", "expert"), None),
            P("expert", None, None),
            P("expert", None, None),
            P("expert", None, None),
        ),
        out_specs=(
            P(("dp", "expert"), None),
            P("expert", "dp", None),
            P("expert", "dp", None),
            P("expert", "dp", None),
        ),
        check_vma=False,
    )
```
